32 devices in a mesh: mem: 2 (over y), gx: 4 (over x, core), gy: 4 (over z).
Axes of the slice: x: 2, y: 2, z: 4, core: 2. Of those that a mesh axis runs over, the one named last changes fastest.
Arguments:
- background_samples: float32 [256, 128, 256], P('mem', 'gx', 'gy'), may hold values from -6 to 6
- measured_space_anomalies: float32 [256, 4, 4, 2048], P('mem', 'gx', 'gy'), may hold values from -32 to 32
- innovation_vector: float32 [4, 4, 2, 1024], P('gx', 'gy', 'mem'), may hold values from -6 to 6
- error_spread_squared: float32 [4, 4, 2, 1024], P('gx', 'gy', 'mem'), may hold values from 0.25 to 4
- measured_nearest_anchor: int32 [4, 4, 2, 1024], P('gx', 'gy', 'mem'), may hold values from 0 to 3
- active_measurement_tally: int32 [4, 4, 2], P('gx', 'gy', 'mem'), may hold values from 256 to 1024, as said below
Outputs:
- updated_sample_matrix: float32 [256, 128, 256], P('mem', 'gx', 'gy')
The draws below stay inside these ranges and needn't reach their ends.
Inputs may be any that keep to these rules, and one draw needn't show every extreme that they name: `active_measurement_tally`: some band has all 1024 slots live and some band only 256.
All inputs are finite; a program needn't handle non-finite values.
Results may differ from the reference program's by a relative error of at most 0.0003.
Values sent between devices are 32-bit elements; how exact they have to be, the bound alone decides.
No kernel may reach another device: no remote copies, remote signals or barrier semaphores. Data moves between devices by JAX's collectives and lax.ppermute only.
A program may use at most 128 MiB of HBM per device.

```python
import math
import jax
import jax.numpy as jnp
from jax import lax

MEMBERSHIP_TOTAL = 256
CGX = 4
NS_STEPS = 12
CB = 32
OBS_DEV = 1024
TX = 4
TY = 4
BANDS = 2
NCX = 16
CROWS = 8
LONGITUDE_CELLS = 128
LATITUDE_CELLS = 256


def draw_active_measurement_tally(key, part):
    cells_total = TX * TY * BANDS
    key_counts, key_full, key_offset = jax.random.split(key, 3)
    counts = jax.random.randint(key_counts, (cells_total,), OBS_DEV // 4, OBS_DEV + 1)
    fullest = jax.random.randint(key_full, (), 0, cells_total)
    offset = jax.random.randint(key_offset, (), 1, cells_total)
    counts = counts.at[fullest].set(OBS_DEV)
    counts = counts.at[(fullest + offset) % cells_total].set(OBS_DEV // 4)
    return counts.reshape(TX, TY, BANDS).astype(jnp.int32)


def draw_measured_space_anomalies(key, part):
    key_noise, key_members, key_slots = jax.random.split(jax.random.fold_in(key, 7), 3)
    mode_count = 2
    jitter = jnp.clip(jax.random.normal(key_noise, (MEMBERSHIP_TOTAL, TX, TY, BANDS, OBS_DEV), jnp.float32), -4.0, 4.0)
    strength = jnp.full((mode_count, 1, TX, TY, BANDS), 4.0, jnp.float32)
    member_pattern = jax.random.uniform(key_members, (mode_count, MEMBERSHIP_TOTAL, TX, TY, BANDS), jnp.float32, -1.7, 1.7) * strength
    slot_pattern = jax.random.uniform(key_slots, (mode_count, TX, TY, BANDS, OBS_DEV), jnp.float32, -1.7, 1.7)
    common = jnp.einsum('rkxyb,rxybo->kxybo', member_pattern, slot_pattern, precision=lax.Precision.HIGHEST)
    combined = jnp.clip(jitter + common, -32.0, 32.0)
    return combined.reshape(MEMBERSHIP_TOTAL, TX, TY, BANDS * OBS_DEV).astype(jnp.float32)


def with_ends(values, own_key, smallest, high):
    longest = values.shape.index(max(values.shape))
    spots = []
    for shift in (0, 1):
        where = [jax.random.randint(jax.random.fold_in(own_key, axis), (), 0, length) for axis, length in enumerate(values.shape)]
        where[longest] = (where[longest] + shift) % values.shape[longest]
        spots.append(tuple(where))
    return values.at[spots[0]].set(smallest).at[spots[1]].set(high)


def block_levels(rng, shape, shards, smallest, largest):
    factor_of = 1.0
    for position, shards_of in shards:
        heights = jax.random.uniform(jax.random.fold_in(jax.random.fold_in(rng, 6), position), (shards_of,), jnp.float32, smallest / len(shards), largest / len(shards))
        factor_of = factor_of * jnp.repeat(jnp.exp(heights), shape[position] // shards_of).reshape((-1,) + (1,) * (len(shape) - 1 - position))
    return factor_of


def normal_values(stream_key, shape, scale, most, cuts=(), kind=jnp.bfloat16):
    array = jax.random.normal(stream_key, shape, jnp.float32) * scale
    if len(cuts) > 0:
        array = block_levels(stream_key, shape, cuts, -0.22, 0.18) * array
    return jnp.clip(array, min=-most, max=most).astype(kind)


def setup_inputs(seed: int = 0) -> dict:
    splits = jax.random.split(jax.random.key(seed), 7)
    return {
        "background_samples": normal_values(splits[0], (MEMBERSHIP_TOTAL, LONGITUDE_CELLS, LATITUDE_CELLS), 1.0, 6.0, ((0, 2), (1, 4), (2, 4)), jnp.float32),
        "measured_space_anomalies": draw_measured_space_anomalies(jax.random.fold_in(splits[6], 71), 0),
        "innovation_vector": normal_values(splits[2], (TX, TY, BANDS, OBS_DEV), 1.0, 6.0, ((0, 4), (1, 4), (2, 2)), jnp.float32),
        "error_spread_squared": jnp.clip(jnp.exp(math.log(4.0) - 2.7725887 * jax.random.uniform(splits[3], (TX, TY, BANDS, OBS_DEV), jnp.float32) ** block_levels(splits[3], (TX, TY, BANDS, OBS_DEV), ((0, 4), (1, 4), (2, 2)), -0.2, 0.2)), 0.25, 4.0),
        "measured_nearest_anchor": with_ends(jax.random.randint(splits[4], (TX, TY, BANDS, OBS_DEV), 0, CGX), jax.random.fold_in(splits[4], 1), 0, CGX - 1).astype(jnp.int32),
        "active_measurement_tally": draw_active_measurement_tally(jax.random.fold_in(splits[6], 71), 0),
    }


precise = lax.Precision.HIGHEST

def transforms_block(obs_block, departure, variance, assign, live_count):
    realization_indices = obs_block.shape[0]
    slots = obs_block.shape[1]
    live_mask = (jnp.arange(slots, dtype=jnp.int32) < live_count).astype(jnp.float32)
    points = jnp.arange(CGX, dtype=jnp.int32)
    distance = (assign[None, :] - points[:, None]).astype(jnp.float32)
    weights = jnp.exp(-0.5 * distance * distance) * live_mask[None, :] / variance[None, :]
    scaled = obs_block[None, :, :] * weights[:, None, :]
    identity = jnp.eye(realization_indices, dtype=jnp.float32)
    covariance = jnp.einsum('pko,jo->pkj', scaled, obs_block, precision=precise) + (realization_indices - 1.0) * identity
    right_side = jnp.einsum('pko,o->pk', scaled, departure, precision=precise)
    frob_norm = jnp.sqrt(lax.optimization_barrier(jnp.sum(covariance * covariance, axis=(1, 2))))
    square_root = covariance / frob_norm[:, None, None]
    inverse = jnp.broadcast_to(identity, covariance.shape)
    for iteration in range(NS_STEPS):
        middle = 1.5 * identity - 0.5 * jnp.einsum('pij,pjk->pik', inverse, square_root, precision=precise)
        square_root = jnp.einsum('pij,pjk->pik', square_root, middle, precision=precise)
        inverse = jnp.einsum('pij,pjk->pik', middle, inverse, precision=precise)
    posterior = jnp.einsum('pij,pjk->pik', inverse, inverse, precision=precise) / frob_norm[:, None, None]
    mean_weights = jnp.einsum('pkj,pj->pk', posterior, right_side, precision=precise)
    return jnp.sqrt(realization_indices - 1.0) * inverse / jnp.sqrt(frob_norm)[:, None, None] + mean_weights[:, :, None]

def tent_x(spacing):
    steps = jnp.arange(2 * spacing, dtype=jnp.float32)
    return 1.0 - jnp.abs(2.0 * steps + 1.0 - 2.0 * spacing) / (2.0 * spacing)

def tent_y(height):
    rows_here = jnp.arange(height, dtype=jnp.float32)
    middle = height // 2
    tent_below = jnp.where(rows_here < middle, (2.0 * middle - 2.0 * rows_here - 1.0) / (2.0 * height), 0.0)
    tent_above = jnp.where(rows_here >= middle, (2.0 * rows_here + 1.0 - 2.0 * middle) / (2.0 * height), 0.0)
    return (tent_below, 1.0 - tent_below - tent_above, tent_above)

def band_delta(transforms, sample_departure_matrix, band_index):
    coarse_cols = transforms.shape[0]
    rows_total = transforms.shape[1]
    realization_indices = sample_departure_matrix.shape[0]
    spacing = sample_departure_matrix.shape[1] // coarse_cols
    band_strip = lax.dynamic_slice_in_dim(sample_departure_matrix, band_index * CB, CB, axis=2)
    rolled = jnp.roll(band_strip, spacing // 2, axis=1).reshape(realization_indices, coarse_cols, spacing, CB)
    windows = jnp.concatenate([rolled, jnp.roll(rolled, -1, axis=1)], axis=2)
    row_ids = (jnp.maximum(band_index - 1, 0), band_index, jnp.minimum(band_index + 1, rows_total - 1))
    weights_x = tent_x(spacing)
    summed = jnp.zeros((coarse_cols, realization_indices, 2 * spacing, CB), jnp.float32)
    for row_id, tent in zip(row_ids, tent_y(CB)):
        picked = lax.dynamic_index_in_dim(transforms, row_id, axis=1, keepdims=False)
        product = jnp.einsum('ckm,kcsy->cmsy', picked, windows, precision=precise)
        summed = summed + product * weights_x[:, None] * tent[None, :]
    cell_blocks = summed[:, :, :spacing] + jnp.roll(summed[:, :, spacing:], 1, axis=0)
    increment_step = cell_blocks.transpose(1, 0, 2, 3).reshape(realization_indices, coarse_cols * spacing, CB)
    return jnp.roll(increment_step, -(spacing // 2), axis=1)

def reference(background_samples, measured_space_anomalies, innovation_vector, error_spread_squared, measured_nearest_anchor, active_measurement_tally):
    realization_indices = background_samples.shape[0]
    background_centroid = lax.optimization_barrier(jnp.mean(background_samples, axis=0))
    sample_departure_matrix = background_samples - background_centroid[None]
    blocks = TX * TY * BANDS
    obs_blocks = measured_space_anomalies.reshape(realization_indices, TX, TY, BANDS, OBS_DEV).transpose(1, 2, 3, 0, 4).reshape(blocks, realization_indices, OBS_DEV)
    inputs = (obs_blocks, innovation_vector.reshape(blocks, OBS_DEV), error_spread_squared.reshape(blocks, OBS_DEV), measured_nearest_anchor.reshape(blocks, OBS_DEV), active_measurement_tally.reshape(blocks))
    transforms = lax.map(lambda values: transforms_block(*values), inputs)
    transforms = transforms.reshape(TX, TY, BANDS, CGX, realization_indices, realization_indices).transpose(0, 3, 1, 2, 4, 5)
    transforms = transforms.reshape(NCX, CROWS, realization_indices, realization_indices)
    deltas = lax.map(lambda band_index: band_delta(transforms, sample_departure_matrix, band_index), jnp.arange(CROWS, dtype=jnp.int32))
    increment_step = deltas.transpose(1, 2, 0, 3).reshape(realization_indices, LONGITUDE_CELLS, LATITUDE_CELLS)
    return background_centroid[None] + increment_step
```

```python
import functools

import jax
import jax.numpy as jnp
from jax import lax
from jax.experimental import pallas as pl
from jax.experimental.pallas import tpu as pltpu
from jax.sharding import PartitionSpec as P

CGX = 4
NS_STEPS = 12
GROUPS = ((0, 1, 2, 3),)

F32 = jnp.float32
BF16 = jnp.bfloat16
VMEM_LIMIT = 56 * 1024 * 1024
NT = (((1,), (1,)), ((), ()))


def dot(a, b):
    return jnp.dot(a, b, preferred_element_type=F32)


def dot_nt(a, b):
    return lax.dot_general(a, b, NT, preferred_element_type=F32)


def split2(x):
    high = x.astype(BF16)
    return high, (x - high.astype(F32)).astype(BF16)


def split3(x):
    high = x.astype(BF16)
    rest = x - high.astype(F32)
    mid = rest.astype(BF16)
    return high, mid, (rest - mid.astype(F32)).astype(BF16)


def mm3(a, b):
    return dot(
        jnp.concatenate([a[0], a[0], a[1]], axis=1),
        jnp.concatenate([b[0], b[1], b[0]], axis=0),
    )


def mm5(a, b):
    return dot(
        jnp.concatenate([a[0], a[1], a[2], a[0], a[1]], axis=1),
        jnp.concatenate([b[0], b[0], b[0], b[1], b[1]], axis=0),
    )


def quartic(p, identity):
    ps = split2(p)
    square = mm3(ps, ps)
    inner = 0.0625 * square - 0.5625 * p + 1.6875 * identity
    return mm3(split2(square), split2(inner)) + (2.25 * identity - 2.4375 * p)


def solve_kernel(points, bands, live_ref, own_ref, *refs):
    others = refs[: bands - 1]
    departure_ref, variance_ref, nearest_ref = refs[bands - 1 : bands + 2]
    outs = refs[bands + 2 : 2 * bands + 2]
    y_ref, cov_ref, right_ref, root_ref, inv_ref = refs[2 * bands + 2 :]
    me = lax.axis_index("mem")
    part, slots = own_ref.shape
    members = y_ref.shape[0]
    for shift, ref in enumerate((own_ref,) + tuple(others)):
        owner = lax.rem(me - shift + bands, bands)
        y_ref[pl.ds(pl.multiple_of(owner * part, part), part), :] = ref[...]
    rows = lax.broadcasted_iota(jnp.int32, (members, members), 0)
    columns = lax.broadcasted_iota(jnp.int32, (members, members), 1)
    identity = (rows == columns).astype(F32)
    live = (lax.broadcasted_iota(jnp.int32, (1, slots), 1) < live_ref[0]).astype(F32)
    base = live * lax.rsqrt(variance_ref[...])
    scales = []
    for g, point in enumerate(points):
        distance = (nearest_ref[...] - point).astype(F32)
        weight = jnp.exp(-0.25 * distance * distance) * base
        y0, y1, y2 = split3(y_ref[...] * weight)
        cross = dot_nt(y0, y1) + dot_nt(y0, y2)
        cov = dot_nt(y0, y0) + dot_nt(y1, y1) + (cross + cross.T)
        cov = cov + (members - 1.0) * identity
        d0, d1 = split2(jnp.broadcast_to(weight * departure_ref[...], (8, slots)))
        right = dot_nt(d0, y0) + dot_nt(d0, y1) + dot_nt(d1, y0)
        right_ref[g] = right
        square_sum = jnp.sum(jnp.sum(cov * cov, axis=1, keepdims=True), axis=0, keepdims=True)
        scale = lax.rsqrt(square_sum)
        scales.append(scale)
        root = cov * scale
        u = split2(quartic(root, identity))
        root_ref[g, 0], root_ref[g, 1], root_ref[g, 2] = split3(mm5(split3(root), u))
        inv_ref[g, 0], inv_ref[g, 1] = u

    def step(_, carry):
        for g in range(len(points)):
            root = (root_ref[g, 0], root_ref[g, 1], root_ref[g, 2])
            inv = (inv_ref[g, 0], inv_ref[g, 1])
            u = split2(quartic(mm3(inv, root), identity))
            root_ref[g, 0], root_ref[g, 1], root_ref[g, 2] = split3(mm5(root, u))
            inv_ref[g, 0], inv_ref[g, 1] = split2(mm3(u, inv))
        return carry

    lax.fori_loop(0, NS_STEPS // 2 - 2, step, 0)
    for g in range(len(points)):
        root = (root_ref[g, 0], root_ref[g, 1])
        inv = (inv_ref[g, 0], inv_ref[g, 1])
        u = split2(quartic(mm3(inv, root), identity))
        last = mm3(u, inv)
        right = right_ref[g, 0:1, :]
        half = jnp.sum(last * right, axis=1, keepdims=True)
        mean_weights = jnp.sum(last * half, axis=0, keepdims=True) * scales[g]
        cov_ref[...] = last * jnp.sqrt((members - 1.0) * scales[g]) + mean_weights
        for shift, out in enumerate(outs):
            target = lax.rem(me + shift, bands)
            out[g] = cov_ref[pl.ds(pl.multiple_of(target * part, part), part), :]


def solve(points, live, own, others, departure, variance, nearest):
    bands = 1 + len(others)
    part, slots = own.shape
    members = part * bands
    count = len(points)
    vmem = pl.BlockSpec(memory_space=pltpu.VMEM)
    return pl.pallas_call(
        functools.partial(solve_kernel, points, bands),
        out_shape=[jax.ShapeDtypeStruct((count, part, members), F32)] * bands,
        in_specs=[pl.BlockSpec(memory_space=pltpu.SMEM)] + [vmem] * (bands + 3),
        out_specs=[vmem] * bands,
        scratch_shapes=[
            pltpu.VMEM((members, slots), F32),
            pltpu.VMEM((members, members), F32),
            pltpu.VMEM((count, 8, members), F32),
            pltpu.VMEM((count, 3, members, members), BF16),
            pltpu.VMEM((count, 2, members, members), BF16),
        ],
        compiler_params=pltpu.CompilerParams(vmem_limit_bytes=VMEM_LIMIT),
        cost_estimate=pl.CostEstimate(
            flops=2 * count * members * members * (4 * slots + 91 * members),
            bytes_accessed=4 * members * (slots + count * members),
            transcendentals=0,
        ),
        name="solve",
    )(live, own, *others, departure, variance, nearest)


def update_kernel(groups, bands, tiles_y, blocks, *refs):
    refs = list(refs)

    def take(n):
        taken, refs[:n] = refs[:n], []
        return taken

    cells = take(blocks)
    rows = [take(bands) for _ in groups]
    ends = [take(bands) for _ in groups]
    row_sides = take(2)
    end_sides = take(2)
    (out,) = take(1)
    x_ref, mean_ref, t_ref = refs
    me = lax.axis_index("mem")
    tile_y = lax.axis_index("gy")
    width, height, _ = out.shape
    part = out.shape[2]
    members = x_ref.shape[3]
    spacing = width // CGX
    depth = height // bands

    def put(slot, column, value):
        t_ref[slot, column, 0], t_ref[slot, column, 1] = split2(value)

    for g, points in enumerate(groups):
        for i, point in enumerate(points):
            for shift in range(bands):
                band = lax.rem(me - shift + bands, bands)
                value = rows[g][shift][i]
                put(band + 1, point + 1, value)

                @pl.when((tile_y == 0) & (band == 0))
                def _(value=value, point=point):
                    put(0, point + 1, value)

                @pl.when((tile_y == tiles_y - 1) & (band == bands - 1))
                def _(value=value, point=point):
                    put(bands + 1, point + 1, value)

                @pl.when((tile_y > 0) & (me == (shift - 1) % bands))
                def _(g=g, i=i, shift=shift, point=point):
                    put(0, point + 1, ends[g][shift][i])

                @pl.when((tile_y < tiles_y - 1) & (me == shift))
                def _(g=g, i=i, shift=shift, point=point):
                    put(bands + 1, point + 1, ends[g][shift][i])

    for side, column in enumerate((0, CGX + 1)):
        for shift in range(bands):
            band = lax.rem(me - shift + bands, bands)
            value = row_sides[side][shift]
            put(band + 1, column, value)

            @pl.when((tile_y == 0) & (band == 0))
            def _(value=value, column=column):
                put(0, column, value)

            @pl.when((tile_y == tiles_y - 1) & (band == bands - 1))
            def _(value=value, column=column):
                put(bands + 1, column, value)

            @pl.when((tile_y > 0) & (me == (shift - 1) % bands))
            def _(side=side, shift=shift, column=column):
                put(0, column, end_sides[side][shift])

            @pl.when((tile_y < tiles_y - 1) & (me == shift))
            def _(side=side, shift=shift, column=column):
                put(bands + 1, column, end_sides[side][shift])

    strip = members // blocks
    total = sum(jnp.sum(ref[...], axis=2, keepdims=True) for ref in cells)
    mean = total * (1.0 / members)
    mean_ref[...] = jnp.broadcast_to(mean, mean_ref.shape)
    for shift, ref in enumerate(cells):
        x0, x1 = split2(ref[...] - mean)
        if blocks == 1:
            x_ref[0], x_ref[1] = x0, x1
        else:
            owner = lax.rem(me - shift + blocks, blocks)
            place = pl.ds(pl.multiple_of(owner * strip, strip), strip)
            x_ref[0, :, :, place] = x0
            x_ref[1, :, :, place] = x1

    for v in range(bands + 1):
        j0, j1 = max(depth * v - depth // 2, 0), min(depth * v + depth // 2, height)
        tall = j1 - j0
        j = lax.broadcasted_iota(jnp.int32, (1, tall, 1), 1).astype(F32) + (
            j0 + 0.5 - (v - 0.5) * depth
        )
        upper = j * (1.0 / depth)
        lower = 1.0 - upper
        for c in range(CGX + 1):
            i0 = max(spacing * c - spacing // 2, 0)
            i1 = min(spacing * c + spacing // 2, width)
            wide = i1 - i0
            x0 = x_ref[0, i0:i1, j0:j1, :].reshape(wide * tall, members)
            x1 = x_ref[1, i0:i1, j0:j1, :].reshape(wide * tall, members)
            left = jnp.concatenate([x0, x0, x1], axis=1)
            i = lax.broadcasted_iota(jnp.int32, (wide, 1, 1), 0).astype(F32) + (
                i0 + 0.5 - (c - 0.5) * spacing
            )
            right_weight = i * (1.0 / spacing)
            result = mean_ref[i0:i1, j0:j1, :part]
            for column, weight in ((c, 1.0 - right_weight), (c + 1, right_weight)):
                t0 = jnp.concatenate([t_ref[v, column, 0], t_ref[v + 1, column, 0]], axis=0)
                t1 = jnp.concatenate([t_ref[v, column, 1], t_ref[v + 1, column, 1]], axis=0)
                product = dot_nt(left, jnp.concatenate([t0, t1, t0], axis=1))
                product = product.reshape(wide, tall, 2 * part)
                result = result + weight * (
                    lower * product[:, :, :part] + upper * product[:, :, part:]
                )
            out[i0:i1, j0:j1, :] = result


def update(groups, tiles_y, cells, rows, ends, row_sides, end_sides, part):
    width, height, strip = cells[0].shape
    bands = len(rows[0])
    members = strip * len(cells)
    vmem = pl.BlockSpec(memory_space=pltpu.VMEM)
    operands = (
        list(cells)
        + [array for group in rows for array in group]
        + [array for group in ends for array in group]
        + list(row_sides)
        + list(end_sides)
    )
    return pl.pallas_call(
        functools.partial(update_kernel, groups, bands, tiles_y, len(cells)),
        out_shape=jax.ShapeDtypeStruct((width, height, part), F32),
        in_specs=[vmem] * len(operands),
        out_specs=vmem,
        scratch_shapes=[
            pltpu.VMEM((2, width, height, members), BF16),
            pltpu.VMEM((width, height, part), F32),
            pltpu.VMEM((bands + 2, CGX + 2, 2, part, members), BF16),
        ],
        compiler_params=pltpu.CompilerParams(vmem_limit_bytes=VMEM_LIMIT),
        cost_estimate=pl.CostEstimate(
            flops=24 * width * height * part * members,
            bytes_accessed=4 * width * height * (members + part),
            transcendentals=0,
        ),
        name="update",
    )(*operands)


def shifted(array, axis, by):
    size = lax.axis_size(axis)
    return lax.ppermute(array, axis, [(i, (i + by) % size) for i in range(size)])


def to_next_tile(array, shift):
    bands = lax.axis_size("mem")
    tiles = lax.axis_size("gy")
    last, first = (shift - 1) % bands, shift
    pairs = [(last * tiles + y, last * tiles + y + 1) for y in range(tiles - 1)]
    pairs += [(first * tiles + y, first * tiles + y - 1) for y in range(1, tiles)]
    return lax.ppermute(array, ("mem", "gy"), pairs)


def per_device(background, anomalies, departure, variance, nearest, tally):
    bands = lax.axis_size("mem")
    me = lax.axis_index("mem")
    part = background.shape[0]
    members = part * bands
    slots = departure.shape[3]
    anomalies = anomalies.reshape(part, bands * slots)
    own = lax.dynamic_slice_in_dim(anomalies, me * slots, slots, axis=1)
    others = []
    for shift in range(1, bands):
        piece = lax.dynamic_slice_in_dim(
            anomalies, lax.rem(me + shift, bands) * slots, slots, axis=1
        )
        others.append(shifted(piece, "mem", shift))
    tile = background.transpose(1, 2, 0)
    cells = [tile] + [shifted(tile, "mem", shift) for shift in range(1, bands)]
    if part % 128:
        order = lax.rem(me - jnp.arange(bands) + bands, bands)
        cells = jnp.take(jnp.stack(cells, axis=2), order, axis=2)
        cells = [cells.reshape(cells.shape[:2] + (members,))]
    rows, ends = [], []
    sides = [None] * CGX
    for points in GROUPS:
        solved = solve(
            points,
            tally.reshape(1),
            own,
            others,
            departure.reshape(1, slots),
            variance.reshape(1, slots),
            nearest.reshape(1, slots),
        )
        row = [solved[0]] + [shifted(solved[s], "mem", s) for s in range(1, bands)]
        end = [to_next_tile(row[s], s) for s in range(bands)]
        rows.append(row)
        ends.append(end)
        for i, point in enumerate(points):
            sides[point] = (
                jnp.stack([array[i] for array in row]),
                jnp.stack([array[i] for array in end]),
            )
    row_sides = [shifted(sides[CGX - 1][0], "gx", 1), shifted(sides[0][0], "gx", -1)]
    end_sides = [shifted(sides[CGX - 1][1], "gx", 1), shifted(sides[0][1], "gx", -1)]
    result = update(
        GROUPS, lax.axis_size("gy"), cells, rows, ends, row_sides, end_sides, part
    )
    return result.transpose(2, 0, 1)


def solution(mesh):
    in_specs = (
        P("mem", "gx", "gy"),
        P("mem", "gx", "gy", None),
        P("gx", "gy", "mem", None),
        P("gx", "gy", "mem", None),
        P("gx", "gy", "mem", None),
        P("gx", "gy", "mem"),
    )
    out_specs = P("mem", "gx", "gy")
    return jax.shard_map(
        per_device, mesh=mesh, in_specs=in_specs, out_specs=out_specs, check_vma=False
    )
```

```python
import functools

import jax
import jax.numpy as jnp
from jax import lax
from jax.experimental import pallas as pl
from jax.experimental.pallas import tpu as pltpu
from jax.sharding import PartitionSpec as P


CGX = 4
NS_STEPS = 12
SIDES = (0, CGX - 1)
POINTS = SIDES + tuple(range(1, CGX - 1))

F32 = jnp.float32
BF16 = jnp.bfloat16
MIB = 1024 * 1024
NT = (((1,), (1,)), ((), ()))


def dot(a, b):
    return jnp.dot(a, b, preferred_element_type=F32)


def dot_nt(a, b):
    return lax.dot_general(a, b, NT, preferred_element_type=F32)


def split2(x):
    high = x.astype(BF16)
    return high, (x - high.astype(F32)).astype(BF16)


def split3(x):
    high = x.astype(BF16)
    rest = x - high.astype(F32)
    mid = rest.astype(BF16)
    return high, mid, (rest - mid.astype(F32)).astype(BF16)


def mm3(a, b):
    return dot(
        jnp.concatenate([a[0], a[0], a[1]], axis=1),
        jnp.concatenate([b[0], b[1], b[0]], axis=0),
    )


def mm5(a, b):
    return dot(
        jnp.concatenate([a[0], a[1], a[2], a[0], a[1]], axis=1),
        jnp.concatenate([b[0], b[0], b[0], b[1], b[1]], axis=0),
    )


def quartics(ps, identity):
    pieces = [split2(p) for p in ps]
    squares = [mm3(piece, piece) for piece in pieces]
    results = []
    for p, square in zip(ps, squares):
        inner = 0.0625 * square - 0.5625 * p + 1.6875 * identity
        results.append((split2(square), split2(inner)))
    results = [mm3(*result) for result in results]
    return [
        split2(result + (2.25 * identity - 2.4375 * p)) for p, result in zip(ps, results)
    ]


def solve_kernel(points, bands, live_ref, own_ref, *refs):
    others = refs[: bands - 1]
    departure_ref, variance_ref, nearest_ref = refs[bands - 1 : bands + 2]
    outs = refs[bands + 2 : 3 * bands + 1]
    y_ref, cov_ref, right_ref, root_ref, inv_ref = refs[3 * bands + 1 :]
    me = lax.axis_index("mem")
    part, slots = own_ref.shape
    members = y_ref.shape[0]
    for shift, ref in enumerate((own_ref,) + tuple(others)):
        owner = lax.rem(me - shift + bands, bands)
        y_ref[pl.ds(pl.multiple_of(owner * part, part), part), :] = ref[...]
    rows = lax.broadcasted_iota(jnp.int32, (members, members), 0)
    columns = lax.broadcasted_iota(jnp.int32, (members, members), 1)
    identity = (rows == columns).astype(F32)
    live = (lax.broadcasted_iota(jnp.int32, (1, slots), 1) < live_ref[0]).astype(F32)
    base = live * lax.rsqrt(variance_ref[...])
    scales, roots = [], []
    for g, point in enumerate(points):
        distance = (nearest_ref[...] - point).astype(F32)
        weight = jnp.exp(-0.25 * distance * distance) * base
        y = split2(y_ref[...] * weight)
        cross = dot_nt(y[0], y[1])
        cov = dot_nt(y[0], y[0]) + dot_nt(y[1], y[1]) + (cross + cross.T)
        cov = cov + (members - 1.0) * identity
        d0, d1 = split2(jnp.broadcast_to(weight * departure_ref[...], (8, slots)))
        right_ref[g] = dot_nt(d0, y[0]) + dot_nt(d0, y[1]) + dot_nt(d1, y[0])
        square_sum = jnp.sum(jnp.sum(cov * cov, axis=1, keepdims=True), axis=0, keepdims=True)
        scale = lax.rsqrt(square_sum)
        scales.append(scale)
        roots.append(cov * scale)
    count = len(points)
    us = quartics(roots, identity)
    for g in range(count):
        for i, piece in enumerate(split3(mm5(split3(roots[g]), us[g]))):
            root_ref[g, i] = piece
        inv_ref[g, 0], inv_ref[g, 1] = us[g]

    def step(_, carry):
        ps = []
        for g in range(count):
            ps.append(mm3((inv_ref[g, 0], inv_ref[g, 1]), (root_ref[g, 0], root_ref[g, 1])))
        us = quartics(ps, identity)
        new = [mm5((root_ref[g, 0], root_ref[g, 1], root_ref[g, 2]), us[g]) for g in range(count)]
        for g in range(count):
            for i, piece in enumerate(split3(new[g])):
                root_ref[g, i] = piece
        new = [mm3(us[g], (inv_ref[g, 0], inv_ref[g, 1])) for g in range(count)]
        for g in range(count):
            inv_ref[g, 0], inv_ref[g, 1] = split2(new[g])
        return carry

    lax.fori_loop(0, NS_STEPS // 2 - 2, step, 0)
    ps = []
    for g in range(count):
        ps.append(mm3((inv_ref[g, 0], inv_ref[g, 1]), (root_ref[g, 0], root_ref[g, 1])))
    us = quartics(ps, identity)
    lasts = [mm3(us[g], (inv_ref[g, 0], inv_ref[g, 1])) for g in range(count)]
    for g in range(count):
        last = lasts[g]
        right = right_ref[g, 0:1, :]
        half = jnp.sum(last * right, axis=1, keepdims=True)
        mean_weights = jnp.sum(last * half, axis=0, keepdims=True) * scales[g]
        cov_ref[...] = last * jnp.sqrt((members - 1.0) * scales[g]) + mean_weights
        for shift in range(bands):
            target = lax.rem(me + shift, bands)
            rows = cov_ref[pl.ds(pl.multiple_of(target * part, part), part), :]
            if shift == 0:
                outs[0][g] = rows
            elif g < 2:
                outs[2 * shift - 1][g] = rows
            else:
                outs[2 * shift][g - 2] = rows


def solve(points, live, own, others, departure, variance, nearest):
    bands = 1 + len(others)
    part, slots = own.shape
    members = part * bands
    count = len(points)
    vmem = pl.BlockSpec(memory_space=pltpu.VMEM)
    return pl.pallas_call(
        functools.partial(solve_kernel, points, bands),
        out_shape=[jax.ShapeDtypeStruct((count, part, members), F32)]
        + [
            jax.ShapeDtypeStruct((n, part, members), F32)
            for _ in others
            for n in (2, count - 2)
        ],
        in_specs=[pl.BlockSpec(memory_space=pltpu.SMEM)] + [vmem] * (bands + 3),
        out_specs=[vmem] * (2 * bands - 1),
        scratch_shapes=[
            pltpu.VMEM((members, slots), F32),
            pltpu.VMEM((members, members), F32),
            pltpu.VMEM((count, 8, members), F32),
            pltpu.VMEM((count, 3, members, members), BF16),
            pltpu.VMEM((count, 2, members, members), BF16),
        ],
        compiler_params=pltpu.CompilerParams(vmem_limit_bytes=32 * MIB),
        cost_estimate=pl.CostEstimate(
            flops=2 * count * members * members * (4 * slots + 91 * members),
            bytes_accessed=4 * members * (slots + count * members),
            transcendentals=0,
        ),
        name="solve",
    )(live, own, *others, departure, variance, nearest)


def prepare_kernel(blocks, *refs):
    cells, (x_ref, mean_ref) = refs[:blocks], refs[blocks:]
    me = lax.axis_index("mem")
    members = x_ref.shape[3]
    strip = members // blocks
    total = sum(jnp.sum(ref[...], axis=2, keepdims=True) for ref in cells)
    mean = total * (1.0 / members)
    mean_ref[...] = jnp.broadcast_to(mean, mean_ref.shape)
    for shift, ref in enumerate(cells):
        x0, x1 = split2(ref[...] - mean)
        if blocks == 1:
            x_ref[0], x_ref[1] = x0, x1
        else:
            owner = lax.rem(me - shift + blocks, blocks)
            place = pl.ds(pl.multiple_of(owner * strip, strip), strip)
            x_ref[0, :, :, place] = x0
            x_ref[1, :, :, place] = x1


def prepare(cells, part):
    width, height, strip = cells[0].shape
    members = strip * len(cells)
    vmem = pl.BlockSpec(memory_space=pltpu.VMEM)
    return pl.pallas_call(
        functools.partial(prepare_kernel, len(cells)),
        out_shape=[
            jax.ShapeDtypeStruct((2, width, height, members), BF16),
            jax.ShapeDtypeStruct((width, height, part), F32),
        ],
        in_specs=[vmem] * len(cells),
        out_specs=[vmem] * 2,
        compiler_params=pltpu.CompilerParams(
            vmem_limit_bytes=16 * width * height * members + 8 * MIB
        ),
        cost_estimate=pl.CostEstimate(
            flops=8 * width * height * members,
            bytes_accessed=8 * width * height * members,
            transcendentals=0,
        ),
        name="prepare",
    )(*cells)


def add_terms(x_ref, t_ref, before_ref, out_ref, bands, mine):
    width, height, part = out_ref.shape
    members = x_ref.shape[3]
    spacing = width // CGX
    depth = height // bands
    for v in range(bands + 1):
        j0, j1 = max(depth * v - depth // 2, 0), min(depth * v + depth // 2, height)
        tall = j1 - j0
        j = lax.broadcasted_iota(jnp.int32, (1, tall, 1), 1).astype(F32) + (
            j0 + 0.5 - (v - 0.5) * depth
        )
        upper = j * (1.0 / depth)
        along_y = (1.0 - upper, upper)
        for c in range(CGX + 1):
            i0 = max(spacing * c - spacing // 2, 0)
            i1 = min(spacing * c + spacing // 2, width)
            wide = i1 - i0
            slots = [(v + a, c + b) for a in (0, 1) for b in (0, 1) if (v + a, c + b) in mine]
            if not slots:
                if before_ref is not out_ref:
                    out_ref[i0:i1, j0:j1, :] = before_ref[i0:i1, j0:j1, :]
                continue
            x0 = x_ref[0, i0:i1, j0:j1, :].reshape(wide * tall, members)
            x1 = x_ref[1, i0:i1, j0:j1, :].reshape(wide * tall, members)
            left = jnp.concatenate([x0, x0, x1], axis=1)
            i = lax.broadcasted_iota(jnp.int32, (wide, 1, 1), 0).astype(F32) + (
                i0 + 0.5 - (c - 0.5) * spacing
            )
            right = i * (1.0 / spacing)
            along_x = (1.0 - right, right)
            t0 = jnp.concatenate([t_ref[mine[slot], 0] for slot in slots], axis=0)
            t1 = jnp.concatenate([t_ref[mine[slot], 1] for slot in slots], axis=0)
            product = dot_nt(left, jnp.concatenate([t0, t1, t0], axis=1))
            product = product.reshape(wide, tall, len(slots) * part)
            result = before_ref[i0:i1, j0:j1, :]
            for n, (row, column) in enumerate(slots):
                weight = along_x[column - c] * along_y[row - v]
                result = result + weight * product[:, :, n * part : (n + 1) * part]
            out_ref[i0:i1, j0:j1, :] = result


def inner_slots(bands):
    names = [(row, column) for row in range(1, bands + 1) for column in range(1, CGX + 1)]
    return {name: n for n, name in enumerate(names)}


def outer_slots(bands):
    names = [(row, column) for row in (0, bands + 1) for column in range(CGX + 2)]
    names += [(row, column) for row in range(1, bands + 1) for column in (0, CGX + 1)]
    return {name: n for n, name in enumerate(names)}


def inner_kernel(bands, *refs):
    x_ref, mean_ref = refs[:2]
    rows = refs[2 : 2 * bands + 1]
    out_ref, t_ref = refs[2 * bands + 1 :]
    me = lax.axis_index("mem")
    for shift in range(bands):
        band = lax.rem(me - shift + bands, bands)
        for n, point in enumerate(POINTS):
            if shift == 0:
                value = rows[0][n]
            elif n < 2:
                value = rows[2 * shift - 1][n]
            else:
                value = rows[2 * shift][n - 2]
            t0, t1 = split2(value)
            t_ref[band * CGX + point, 0] = t0
            t_ref[band * CGX + point, 1] = t1
    add_terms(x_ref, t_ref, mean_ref, out_ref, bands, inner_slots(bands))


def outer_kernel(bands, tiles_y, *refs):
    refs = list(refs)

    def take(n):
        taken, refs[:n] = refs[:n], []
        return taken

    x_ref, before_ref = take(2)
    (own,) = take(1)
    ends_side = take(bands - 1)
    ends_mid = take(bands - 1)
    other_side = take(bands - 1)
    other_mid = take(bands - 1)
    (own_end,) = take(1)
    row_sides = take(2)
    end_sides = take(2)
    out_ref, t_ref = refs
    me = lax.axis_index("mem")
    tile_y = lax.axis_index("gy")
    slots = outer_slots(bands)
    south, north = slots[0, 0], slots[bands + 1, 0]

    def put(slot, value):
        t0, t1 = split2(value)
        t_ref[slot, 0] = t0
        t_ref[slot, 1] = t1

    def put_ends(shift, column, tile_value, end_value):
        band = lax.rem(me - shift + bands, bands)

        @pl.when((tile_y == 0) & (band == 0))
        def _():
            put(south + column, tile_value())

        @pl.when((tile_y == tiles_y - 1) & (band == bands - 1))
        def _():
            put(north + column, tile_value())

        @pl.when((tile_y > 0) & (me == (shift - 1) % bands))
        def _():
            put(south + column, end_value())

        @pl.when((tile_y < tiles_y - 1) & (me == shift))
        def _():
            put(north + column, end_value())

    for shift in range(bands):
        band = lax.rem(me - shift + bands, bands)
        for n, point in enumerate(POINTS):
            if shift == 0:
                here, there, k = own, own_end, n
            elif n < 2:
                here, there, k = other_side[shift - 1], ends_side[shift - 1], n
            else:
                here, there, k = other_mid[shift - 1], ends_mid[shift - 1], n - 2
            put_ends(
                shift,
                point + 1,
                lambda here=here, k=k: here[k],
                lambda there=there, k=k: there[k],
            )
        for side, column in enumerate((0, CGX + 1)):
            put(slots[1, 0] + 2 * band + side, row_sides[side][shift])
            put_ends(
                shift,
                column,
                lambda side=side: row_sides[side][shift],
                lambda side=side: end_sides[side][shift],
            )
    add_terms(x_ref, t_ref, before_ref, out_ref, bands, slots)


def apply_terms(kernel, x, before, operands, slots, flops):
    _, width, height, members = x.shape
    part = before.shape[2]
    vmem = pl.BlockSpec(memory_space=pltpu.VMEM)
    size = sum(array.size for array in operands)
    return pl.pallas_call(
        kernel,
        out_shape=jax.ShapeDtypeStruct((width, height, part), F32),
        in_specs=[vmem] * (2 + len(operands)),
        out_specs=vmem,
        scratch_shapes=[pltpu.VMEM((len(slots), 2, part, members), BF16)],
        compiler_params=pltpu.CompilerParams(
            vmem_limit_bytes=min(4 * (x.size + 2 * before.size + 2 * size) + 8 * MIB, 60 * MIB)
        ),
        cost_estimate=pl.CostEstimate(
            flops=flops, bytes_accessed=4 * (x.size + before.size), transcendentals=0
        ),
    )(x, before, *operands)


def shifted(array, axis, by):
    size = lax.axis_size(axis)
    return lax.ppermute(array, axis, [(i, (i + by) % size) for i in range(size)])


def to_next_tile(array, shift):
    bands = lax.axis_size("mem")
    tiles = lax.axis_size("gy")
    last, first = (shift - 1) % bands, shift
    pairs = [(last * tiles + y, last * tiles + y + 1) for y in range(tiles - 1)]
    pairs += [(first * tiles + y, first * tiles + y - 1) for y in range(1, tiles)]
    return lax.ppermute(array, ("mem", "gy"), pairs)


def analysis(background, anomalies, departure, variance, nearest, tally):
    bands = lax.axis_size("mem")
    tiles_y = lax.axis_size("gy")
    me = lax.axis_index("mem")
    part = background.shape[0]
    members = part * bands
    slots = departure.shape[3]
    anomalies = anomalies.reshape(part, bands * slots)
    others = []
    for shift in range(1, bands):
        piece = lax.dynamic_slice_in_dim(
            anomalies, lax.rem(me + shift, bands) * slots, slots, axis=1
        )
        others.append(shifted(piece, "mem", shift))
    own = lax.dynamic_slice_in_dim(anomalies, me * slots, slots, axis=1)
    tile = background.transpose(1, 2, 0)
    cells = [tile]
    for shift in range(1, bands):
        cells.append(shifted(tile, "mem", shift))
    if part % 128:
        order = lax.rem(me - jnp.arange(bands) + bands, bands)
        cells = jnp.take(jnp.stack(cells, axis=2), order, axis=2)
        cells = [cells.reshape(cells.shape[:2] + (members,))]
    solved = solve(
        POINTS,
        tally.reshape(1),
        own,
        others,
        departure.reshape(1, slots),
        variance.reshape(1, slots),
        nearest.reshape(1, slots),
    )
    row = solved[0]
    other_side = [shifted(solved[2 * s - 1], "mem", s) for s in range(1, bands)]
    own_end = to_next_tile(row, 0)
    other_mid = [shifted(solved[2 * s], "mem", s) for s in range(1, bands)]
    ends_side = [to_next_tile(other_side[s - 1], s) for s in range(1, bands)]
    row_sides = [
        shifted(jnp.stack([row[n]] + [array[n] for array in other_side]), "gx", by)
        for n, by in ((1, 1), (0, -1))
    ]
    ends_mid = [to_next_tile(other_mid[s - 1], s) for s in range(1, bands)]
    end_sides = [
        shifted(jnp.stack([own_end[n]] + [array[n] for array in ends_side]), "gx", by)
        for n, by in ((1, 1), (0, -1))
    ]
    x, mean = prepare(cells, part)
    operands = [row]
    for side, mid in zip(other_side, other_mid):
        operands += [side, mid]
    work = 6 * mean.size * members
    result = apply_terms(
        functools.partial(inner_kernel, bands),
        x,
        mean,
        operands,
        inner_slots(bands),
        3 * work,
    )
    result = apply_terms(
        functools.partial(outer_kernel, bands, tiles_y),
        x,
        result,
        [row]
        + ends_side
        + ends_mid
        + other_side
        + other_mid
        + [own_end]
        + row_sides
        + end_sides,
        outer_slots(bands),
        work,
    )
    return result.transpose(2, 0, 1)


def solution(mesh):
    in_specs = (
        P("mem", "gx", "gy"),
        P("mem", "gx", "gy", None),
        P("gx", "gy", "mem", None),
        P("gx", "gy", "mem", None),
        P("gx", "gy", "mem", None),
        P("gx", "gy", "mem"),
    )
    out_specs = P("mem", "gx", "gy")
    return jax.shard_map(
        analysis, mesh=mesh, in_specs=in_specs, out_specs=out_specs, check_vma=False
    )
```

```python
import functools

import jax
import jax.numpy as jnp
from jax import lax
from jax.experimental import pallas as pl
from jax.experimental.pallas import tpu as pltpu
from jax.sharding import PartitionSpec as P


CGX = 4
NS_STEPS = 12
SIDES = (0, CGX - 1)
POINTS = SIDES + tuple(range(1, CGX - 1))

F32 = jnp.float32
BF16 = jnp.bfloat16
MIB = 1024 * 1024
NT = (((1,), (1,)), ((), ()))


def dot(a, b):
    return jnp.dot(a, b, preferred_element_type=F32)


def dot_nt(a, b):
    return lax.dot_general(a, b, NT, preferred_element_type=F32)


def split2(x):
    high = x.astype(BF16)
    return high, (x - high.astype(F32)).astype(BF16)


def split3(x):
    high = x.astype(BF16)
    rest = x - high.astype(F32)
    mid = rest.astype(BF16)
    return high, mid, (rest - mid.astype(F32)).astype(BF16)


def mm3(a, b):
    return dot(
        jnp.concatenate([a[0], a[0], a[1]], axis=1),
        jnp.concatenate([b[0], b[1], b[0]], axis=0),
    )


def mm5(a, b):
    return dot(
        jnp.concatenate([a[0], a[1], a[2], a[0], a[1]], axis=1),
        jnp.concatenate([b[0], b[0], b[0], b[1], b[1]], axis=0),
    )


def mm1(a, b):
    return dot(a[0], b[0])


def quartics(ps, identity, square_mm, inner_mm):
    squares = [square_mm(piece, piece) for piece in [split2(p) for p in ps]]
    inner = [
        inner_mm(split2(square), split2(0.0625 * square - 0.5625 * p))
        for p, square in zip(ps, squares)
    ]
    return [
        split2(product + (1.6875 * square + (2.25 * identity - 2.4375 * p)))
        for p, square, product in zip(ps, squares, inner)
    ]


def solve_kernel(points, bands, live_ref, own_ref, *refs):
    others = refs[: bands - 1]
    departure_ref, variance_ref, nearest_ref = refs[bands - 1 : bands + 2]
    outs = refs[bands + 2 : 3 * bands + 1]
    y_ref, cov_ref, right_ref, root_ref, inv_ref = refs[3 * bands + 1 :]
    me = lax.axis_index("mem")
    part, slots = own_ref.shape
    members = y_ref.shape[0]
    for shift, ref in enumerate((own_ref,) + tuple(others)):
        owner = lax.rem(me - shift + bands, bands)
        y_ref[pl.ds(pl.multiple_of(owner * part, part), part), :] = ref[...]
    rows = lax.broadcasted_iota(jnp.int32, (members, members), 0)
    columns = lax.broadcasted_iota(jnp.int32, (members, members), 1)
    identity = (rows == columns).astype(F32)
    live = (lax.broadcasted_iota(jnp.int32, (1, slots), 1) < live_ref[0]).astype(F32)
    base = live * lax.rsqrt(variance_ref[...])
    scales, roots = [], []
    for g, point in enumerate(points):
        distance = (nearest_ref[...] - point).astype(F32)
        weight = jnp.exp(-0.25 * distance * distance) * base
        y = split2(y_ref[...] * weight)
        cross = dot_nt(y[0], y[1])
        cov = dot_nt(y[0], y[0]) + dot_nt(y[1], y[1]) + (cross + cross.T)
        cov = cov + (members - 1.0) * identity
        d0, d1 = split2(jnp.broadcast_to(weight * departure_ref[...], (8, slots)))
        right_ref[g] = dot_nt(d0, y[0]) + dot_nt(d0, y[1]) + dot_nt(d1, y[0])
        square_sum = jnp.sum(jnp.sum(cov * cov, axis=1, keepdims=True), axis=0, keepdims=True)
        scale = lax.rsqrt(square_sum)
        scales.append(scale)
        roots.append(cov * scale)
    count = len(points)
    us = quartics(roots, identity, mm1, mm1)
    for g in range(count):
        for i, piece in enumerate(split3(mm5(split3(roots[g]), us[g]))):
            root_ref[g, i] = piece
        inv_ref[g, 0], inv_ref[g, 1] = us[g]

    def products():
        return [
            mm3((inv_ref[g, 0], inv_ref[g, 1]), (root_ref[g, 0], root_ref[g, 1]))
            for g in range(count)
        ]

    def inverses(us):
        return [mm3(us[g], (inv_ref[g, 0], inv_ref[g, 1])) for g in range(count)]

    def step(square_mm, full):
        us = quartics(products(), identity, square_mm, mm1)
        if full:
            new = [
                mm5((root_ref[g, 0], root_ref[g, 1], root_ref[g, 2]), us[g])
                for g in range(count)
            ]
        else:
            new = [mm3((root_ref[g, 0], root_ref[g, 1]), us[g]) for g in range(count)]
        for g in range(count):
            pieces = split3(new[g]) if full else split2(new[g])
            for i, piece in enumerate(pieces):
                root_ref[g, i] = piece
        new = inverses(us)
        for g in range(count):
            inv_ref[g, 0], inv_ref[g, 1] = split2(new[g])

    def early(_, carry):
        step(mm1, True)
        return carry

    lax.fori_loop(0, NS_STEPS // 2 - 3, early, 0)
    step(mm3, False)
    lasts = inverses(quartics(products(), identity, mm3, mm3))
    for g in range(count):
        last = lasts[g]
        right = right_ref[g, 0:1, :]
        half = jnp.sum(last * right, axis=1, keepdims=True)
        mean_weights = jnp.sum(last * half, axis=0, keepdims=True) * scales[g]
        cov_ref[...] = last * jnp.sqrt((members - 1.0) * scales[g]) + mean_weights
        for shift in range(bands):
            target = lax.rem(me + shift, bands)
            rows = cov_ref[pl.ds(pl.multiple_of(target * part, part), part), :]
            if shift == 0:
                outs[0][g] = rows
            elif g < 2:
                outs[2 * shift - 1][g] = rows
            else:
                outs[2 * shift][g - 2] = rows


def solve(points, live, own, others, departure, variance, nearest):
    bands = 1 + len(others)
    part, slots = own.shape
    members = part * bands
    count = len(points)
    vmem = pl.BlockSpec(memory_space=pltpu.VMEM)
    return pl.pallas_call(
        functools.partial(solve_kernel, points, bands),
        out_shape=[jax.ShapeDtypeStruct((count, part, members), F32)]
        + [
            jax.ShapeDtypeStruct((n, part, members), F32)
            for _ in others
            for n in (2, count - 2)
        ],
        in_specs=[pl.BlockSpec(memory_space=pltpu.SMEM)] + [vmem] * (bands + 3),
        out_specs=[vmem] * (2 * bands - 1),
        scratch_shapes=[
            pltpu.VMEM((members, slots), F32),
            pltpu.VMEM((members, members), F32),
            pltpu.VMEM((count, 8, members), F32),
            pltpu.VMEM((count, 3, members, members), BF16),
            pltpu.VMEM((count, 2, members, members), BF16),
        ],
        compiler_params=pltpu.CompilerParams(vmem_limit_bytes=32 * MIB),
        cost_estimate=pl.CostEstimate(
            flops=2 * count * members * members * (3 * slots + 71 * members),
            bytes_accessed=4 * members * (slots + count * members),
            transcendentals=0,
        ),
        name="solve",
    )(live, own, *others, departure, variance, nearest)


def prepare_kernel(blocks, *refs):
    me = lax.axis_index("mem")
    cells, edges = refs[:blocks], refs[blocks : 2 * blocks]
    x_ref, mean_ref, edge_ref = refs[2 * blocks :]
    members = x_ref.shape[3]
    strip = members // blocks
    for pieces, to_ref in ((cells, x_ref), (edges, edge_ref)):
        total = sum(jnp.sum(ref[...], axis=2, keepdims=True) for ref in pieces)
        mean = total * (1.0 / members)
        if to_ref is x_ref:
            mean_ref[...] = jnp.broadcast_to(mean, mean_ref.shape)
        for shift, ref in enumerate(pieces):
            x0, x1 = split2(ref[...] - mean)
            if blocks == 1:
                to_ref[0], to_ref[1] = x0, x1
            else:
                owner = lax.rem(me - shift + blocks, blocks)
                place = pl.ds(pl.multiple_of(owner * strip, strip), strip)
                to_ref[0, :, :, place] = x0
                to_ref[1, :, :, place] = x1


def prepare(cells, edges, part):
    width, height, strip = cells[0].shape
    members = strip * len(cells)
    vmem = pl.BlockSpec(memory_space=pltpu.VMEM)
    return pl.pallas_call(
        functools.partial(prepare_kernel, len(cells)),
        out_shape=[
            jax.ShapeDtypeStruct((2, width, height, members), BF16),
            jax.ShapeDtypeStruct((width, height, part), F32),
            jax.ShapeDtypeStruct((2,) + edges[0].shape[:2] + (members,), BF16),
        ],
        in_specs=[vmem] * (2 * len(cells)),
        out_specs=[vmem] * 3,
        compiler_params=pltpu.CompilerParams(
            vmem_limit_bytes=16 * width * height * members + 8 * MIB
        ),
        cost_estimate=pl.CostEstimate(
            flops=8 * width * height * members,
            bytes_accessed=8 * width * height * members,
            transcendentals=0,
        ),
        name="prepare",
    )(*cells, *edges)


def add_terms(x_ref, t_ref, before_ref, out_ref, bands, mine):
    width, height, part = out_ref.shape
    members = x_ref.shape[3]
    spacing = width // CGX
    depth = height // bands
    for v in range(bands + 1):
        j0, j1 = max(depth * v - depth // 2, 0), min(depth * v + depth // 2, height)
        tall = j1 - j0
        j = lax.broadcasted_iota(jnp.int32, (1, tall, 1), 1).astype(F32) + (
            j0 + 0.5 - (v - 0.5) * depth
        )
        upper = j * (1.0 / depth)
        along_y = (1.0 - upper, upper)
        for c in range(CGX + 1):
            i0 = max(spacing * c - spacing // 2, 0)
            i1 = min(spacing * c + spacing // 2, width)
            wide = i1 - i0
            slots = [(v + a, c + b) for a in (0, 1) for b in (0, 1) if (v + a, c + b) in mine]
            if not slots:
                if before_ref is not out_ref:
                    out_ref[i0:i1, j0:j1, :] = before_ref[i0:i1, j0:j1, :]
                continue
            x0 = x_ref[0, i0:i1, j0:j1, :].reshape(wide * tall, members)
            x1 = x_ref[1, i0:i1, j0:j1, :].reshape(wide * tall, members)
            left = jnp.concatenate([x0, x0, x1], axis=1)
            i = lax.broadcasted_iota(jnp.int32, (wide, 1, 1), 0).astype(F32) + (
                i0 + 0.5 - (c - 0.5) * spacing
            )
            right = i * (1.0 / spacing)
            along_x = (1.0 - right, right)
            t0 = jnp.concatenate([t_ref[mine[slot], 0] for slot in slots], axis=0)
            t1 = jnp.concatenate([t_ref[mine[slot], 1] for slot in slots], axis=0)
            product = dot_nt(left, jnp.concatenate([t0, t1, t0], axis=1))
            product = product.reshape(wide, tall, len(slots) * part)
            result = before_ref[i0:i1, j0:j1, :]
            for n, (row, column) in enumerate(slots):
                weight = along_x[column - c] * along_y[row - v]
                result = result + weight * product[:, :, n * part : (n + 1) * part]
            out_ref[i0:i1, j0:j1, :] = result


def inner_slots(bands):
    names = [(row, column) for row in range(1, bands + 1) for column in range(1, CGX + 1)]
    return {name: n for n, name in enumerate(names)}


def edge_slots(bands):
    names = [(row, column) for row in (0, bands + 1) for column in (1, CGX)]
    names += [(row, column) for row in range(1, bands + 1) for column in (0, CGX + 1)]
    return {name: n for n, name in enumerate(names)}


def last_slots(bands):
    names = [(row, column) for row in (0, bands + 1) for column in range(2, CGX)]
    return {name: n for n, name in enumerate(names)}


def put(t_ref, slot, value):
    t0, t1 = split2(value)
    t_ref[slot, 0] = t0
    t_ref[slot, 1] = t1


def put_ends(t_ref, south, north, bands, tiles_y, shift, tile_value, end_value):
    me = lax.axis_index("mem")
    tile_y = lax.axis_index("gy")
    band = lax.rem(me - shift + bands, bands)

    @pl.when((tile_y == 0) & (band == 0))
    def _():
        put(t_ref, south, tile_value())

    @pl.when((tile_y == tiles_y - 1) & (band == bands - 1))
    def _():
        put(t_ref, north, tile_value())

    @pl.when((tile_y > 0) & (me == (shift - 1) % bands))
    def _():
        put(t_ref, south, end_value())

    @pl.when((tile_y < tiles_y - 1) & (me == shift))
    def _():
        put(t_ref, north, end_value())


def inner_kernel(bands, *refs):
    x_ref, mean_ref = refs[:2]
    rows = refs[2 : 2 * bands + 1]
    out_ref, t_ref = refs[2 * bands + 1 :]
    me = lax.axis_index("mem")
    for shift in range(bands):
        band = lax.rem(me - shift + bands, bands)
        for n, point in enumerate(POINTS):
            if shift == 0:
                value = rows[0][n]
            elif n < 2:
                value = rows[2 * shift - 1][n]
            else:
                value = rows[2 * shift][n - 2]
            t0, t1 = split2(value)
            t_ref[band * CGX + point, 0] = t0
            t_ref[band * CGX + point, 1] = t1
    add_terms(x_ref, t_ref, mean_ref, out_ref, bands, inner_slots(bands))


def edge_kernel(bands, tiles_y, *refs):
    refs = list(refs)

    def take(n):
        taken, refs[:n] = refs[:n], []
        return taken

    x_ref, before_ref = take(2)
    rows, ends, sides = take(bands), take(bands), take(2)
    out_ref, t_ref = refs
    me = lax.axis_index("mem")
    slots = edge_slots(bands)
    for shift in range(bands):
        band = lax.rem(me - shift + bands, bands)
        for n, point in enumerate(SIDES):
            put_ends(
                t_ref,
                slots[0, point + 1],
                slots[bands + 1, point + 1],
                bands,
                tiles_y,
                shift,
                lambda shift=shift, n=n: rows[shift][n],
                lambda shift=shift, n=n: ends[shift][n],
            )
        for side in (0, 1):
            put(t_ref, slots[1, 0] + 2 * band + side, sides[side][shift])
    add_terms(x_ref, t_ref, before_ref, out_ref, bands, slots)


def corner_kernel(bands, tiles_y, spacing, depth, *refs):
    edge_ref = refs[0]
    rows, ends = refs[1 : 1 + bands], refs[1 + bands : 1 + 2 * bands]
    left_ref, right_ref, t_ref = refs[1 + 2 * bands :]
    members = edge_ref.shape[3]
    part = left_ref.shape[2]
    for shift in range(bands):
        for n in (0, 1):
            put_ends(
                t_ref,
                n,
                2 + n,
                bands,
                tiles_y,
                shift,
                lambda shift=shift, n=n: rows[shift][n],
                lambda shift=shift, n=n: ends[shift][n],
            )
    half, tall = spacing // 2, depth // 2
    i = lax.broadcasted_iota(jnp.int32, (half, 1, 1), 0).astype(F32) + 0.5
    j = lax.broadcasted_iota(jnp.int32, (1, tall, 1), 1).astype(F32) + 0.5
    along_x = (i * (1.0 / spacing), 0.5 - i * (1.0 / spacing))
    along_y = (0.5 - j * (1.0 / depth), j * (1.0 / depth))
    for n, out_ref in enumerate((left_ref, right_ref)):
        for end in (0, 1):
            cells = slice(end * tall, (end + 1) * tall)
            first = 0 if n else half
            x0 = edge_ref[0, first : first + half, cells, :].reshape(half * tall, members)
            x1 = edge_ref[1, first : first + half, cells, :].reshape(half * tall, members)
            slot = 2 * end + n
            product = dot_nt(
                jnp.concatenate([x0, x0, x1], axis=1),
                jnp.concatenate([t_ref[slot, 0], t_ref[slot, 1], t_ref[slot, 0]], axis=1),
            )
            out_ref[:, cells, :] = (
                along_x[n] * along_y[end] * product.reshape(half, tall, part)
            )


def corners(bands, tiles_y, spacing, depth, edge, rows, ends):
    part, members = rows[0].shape[1:]
    vmem = pl.BlockSpec(memory_space=pltpu.VMEM)
    shape = jax.ShapeDtypeStruct((spacing // 2, depth, part), F32)
    return pl.pallas_call(
        functools.partial(corner_kernel, bands, tiles_y, spacing, depth),
        out_shape=[shape] * 2,
        in_specs=[vmem] * (1 + 2 * bands),
        out_specs=[vmem] * 2,
        scratch_shapes=[pltpu.VMEM((4, 2, part, members), BF16)],
        compiler_params=pltpu.CompilerParams(vmem_limit_bytes=16 * MIB),
        cost_estimate=pl.CostEstimate(
            flops=12 * spacing * depth * part * members,
            bytes_accessed=16 * part * members,
            transcendentals=0,
        ),
        name="corners",
    )(edge, *rows, *ends)


def last_kernel(bands, tiles_y, *refs):
    refs = list(refs)

    def take(n):
        taken, refs[:n] = refs[:n], []
        return taken

    x_ref, before_ref = take(2)
    rows, ends, given = take(bands), take(bands), take(2)
    out_ref, t_ref = refs
    slots = last_slots(bands)
    for shift in range(bands):
        for n in range(CGX - 2):
            k = 2 + n if shift == 0 else n
            put_ends(
                t_ref,
                slots[0, 2 + n],
                slots[bands + 1, 2 + n],
                bands,
                tiles_y,
                shift,
                lambda shift=shift, k=k: rows[shift][k],
                lambda shift=shift, k=k: ends[shift][k],
            )
    add_terms(x_ref, t_ref, before_ref, out_ref, bands, slots)
    width, height, _ = out_ref.shape
    half, depth, _ = given[0].shape
    for ref, first in zip(given, (0, width - half)):
        for start, cells in ((0, 0), (depth // 2, height - depth // 2)):
            place = slice(cells, cells + depth // 2)
            out_ref[first : first + half, place, :] = (
                before_ref[first : first + half, place, :]
                + ref[:, start : start + depth // 2, :]
            )


def apply_terms(kernel, x, before, operands, slots, flops):
    _, width, height, members = x.shape
    part = before.shape[2]
    vmem = pl.BlockSpec(memory_space=pltpu.VMEM)
    size = sum(array.size for array in operands)
    return pl.pallas_call(
        kernel,
        out_shape=jax.ShapeDtypeStruct((width, height, part), F32),
        in_specs=[vmem] * (2 + len(operands)),
        out_specs=vmem,
        scratch_shapes=[pltpu.VMEM((len(slots), 2, part, members), BF16)],
        compiler_params=pltpu.CompilerParams(
            vmem_limit_bytes=min(4 * (x.size + 2 * before.size + 2 * size) + 8 * MIB, 60 * MIB)
        ),
        cost_estimate=pl.CostEstimate(
            flops=flops, bytes_accessed=4 * (x.size + before.size), transcendentals=0
        ),
    )(x, before, *operands)


def shifted(array, axis, by):
    size = lax.axis_size(axis)
    return lax.ppermute(array, axis, [(i, (i + by) % size) for i in range(size)])


def to_next_tile(array, shift):
    bands = lax.axis_size("mem")
    tiles = lax.axis_size("gy")
    last, first = (shift - 1) % bands, shift
    pairs = [(last * tiles + y, last * tiles + y + 1) for y in range(tiles - 1)]
    pairs += [(first * tiles + y, first * tiles + y - 1) for y in range(1, tiles)]
    return lax.ppermute(array, ("mem", "gy"), pairs)


def analysis(background, anomalies, departure, variance, nearest, tally):
    bands = lax.axis_size("mem")
    tiles_y = lax.axis_size("gy")
    me = lax.axis_index("mem")
    part = background.shape[0]
    members = part * bands
    slots = departure.shape[3]
    anomalies = anomalies.reshape(part, bands * slots)
    others = []
    for shift in range(1, bands):
        piece = lax.dynamic_slice_in_dim(
            anomalies, lax.rem(me + shift, bands) * slots, slots, axis=1
        )
        others.append(piece)
    anomalies, others = lax.optimization_barrier((anomalies, others))
    others = [shifted(piece, "mem", s) for s, piece in enumerate(others, 1)]
    own = lax.dynamic_slice_in_dim(anomalies, me * slots, slots, axis=1)
    tile = background.transpose(1, 2, 0)
    width, height = tile.shape[:2]
    spacing, depth = width // CGX, height // bands
    ends_y = jnp.concatenate([tile[:, : depth // 2], tile[:, height - depth // 2 :]], axis=1)
    edge = jnp.concatenate(
        [
            shifted(ends_y[: spacing // 2], "gx", -1),
            shifted(ends_y[width - spacing // 2 :], "gx", 1),
        ],
        axis=0,
    )

    def gathered(array):
        blocks = [array]
        for shift in range(1, bands):
            blocks.append(shifted(array, "mem", shift))
        if part % 128:
            order = lax.rem(me - jnp.arange(bands) + bands, bands)
            blocks = jnp.take(jnp.stack(blocks, axis=2), order, axis=2)
            blocks = [blocks.reshape(blocks.shape[:2] + (members,))]
        return blocks

    cells = gathered(tile)
    edges = gathered(edge)
    solved = solve(
        POINTS,
        tally.reshape(1),
        own,
        others,
        departure.reshape(1, slots),
        variance.reshape(1, slots),
        nearest.reshape(1, slots),
    )
    row = solved[0]
    other_side = [shifted(solved[2 * s - 1], "mem", s) for s in range(1, bands)]
    other_mid = [shifted(solved[2 * s], "mem", s) for s in range(1, bands)]
    own_end = to_next_tile(row, 0)
    ends_side = [to_next_tile(other_side[s - 1], s) for s in range(1, bands)]
    row_sides = [
        shifted(jnp.stack([row[n]] + [array[n] for array in other_side]), "gx", by)
        for n, by in ((1, 1), (0, -1))
    ]
    ends_mid = [to_next_tile(other_mid[s - 1], s) for s in range(1, bands)]
    x, mean, edge = prepare(cells, edges, part)
    left, right = corners(
        bands, tiles_y, spacing, depth, edge, [row] + other_side, [own_end] + ends_side
    )
    given = [shifted(right, "gx", 1), shifted(left, "gx", -1)]
    operands = [row]
    for side, mid in zip(other_side, other_mid):
        operands += [side, mid]
    work = 6 * mean.size * members
    result = apply_terms(
        functools.partial(inner_kernel, bands),
        x,
        mean,
        operands,
        inner_slots(bands),
        3 * work,
    )
    result = apply_terms(
        functools.partial(edge_kernel, bands, tiles_y),
        x,
        result,
        [row] + other_side + [own_end] + ends_side + row_sides,
        edge_slots(bands),
        work,
    )
    result = apply_terms(
        functools.partial(last_kernel, bands, tiles_y),
        x,
        result,
        [row] + other_mid + [own_end] + ends_mid + given,
        last_slots(bands),
        work // 2,
    )
    return result.transpose(2, 0, 1)


def solution(mesh):
    in_specs = (
        P("mem", "gx", "gy"),
        P("mem", "gx", "gy", None),
        P("gx", "gy", "mem", None),
        P("gx", "gy", "mem", None),
        P("gx", "gy", "mem", None),
        P("gx", "gy", "mem"),
    )
    out_specs = P("mem", "gx", "gy")
    return jax.shard_map(
        analysis, mesh=mesh, in_specs=in_specs, out_specs=out_specs, check_vma=False
    )
```

```python
import functools

import jax
import jax.numpy as jnp
from jax import lax
from jax.experimental import pallas as pl
from jax.experimental.pallas import tpu as pltpu
from jax.sharding import PartitionSpec as P


CGX = 4
NS_STEPS = 12
SIDES = (0, CGX - 1)
POINTS = SIDES + tuple(range(1, CGX - 1))

F32 = jnp.float32
BF16 = jnp.bfloat16
MIB = 1024 * 1024
NT = (((1,), (1,)), ((), ()))


def dot(a, b):
    return jnp.dot(a, b, preferred_element_type=F32)


def dot_nt(a, b):
    return lax.dot_general(a, b, NT, preferred_element_type=F32)


def split2(x):
    high = x.astype(BF16)
    return high, (x - high.astype(F32)).astype(BF16)


def split3(x):
    high = x.astype(BF16)
    rest = x - high.astype(F32)
    mid = rest.astype(BF16)
    return high, mid, (rest - mid.astype(F32)).astype(BF16)


def mm3(a, b):
    return dot(
        jnp.concatenate([a[0], a[0], a[1]], axis=1),
        jnp.concatenate([b[0], b[1], b[0]], axis=0),
    )


def mm5(a, b):
    return dot(
        jnp.concatenate([a[0], a[1], a[2], a[0], a[1]], axis=1),
        jnp.concatenate([b[0], b[0], b[0], b[1], b[1]], axis=0),
    )


def mm1(a, b):
    return dot(a[0], b[0])


def quartics(ps, identity, square_mm, inner_mm):
    squares = [square_mm(piece, piece) for piece in [split2(p) for p in ps]]
    inner = [
        inner_mm(split2(square), split2(0.0625 * square - 0.5625 * p))
        for p, square in zip(ps, squares)
    ]
    return [
        split2(product + (1.6875 * square + (2.25 * identity - 2.4375 * p)))
        for p, square, product in zip(ps, squares, inner)
    ]


def solve_kernel(points, bands, live_ref, own_ref, *refs):
    others = refs[: bands - 1]
    departure_ref, variance_ref, nearest_ref = refs[bands - 1 : bands + 2]
    outs = refs[bands + 2 : 3 * bands + 1]
    y_ref, cov_ref, right_ref, root_ref, inv_ref = refs[3 * bands + 1 :]
    me = lax.axis_index("mem")
    part, slots = own_ref.shape
    members = y_ref.shape[0]
    for shift, ref in enumerate((own_ref,) + tuple(others)):
        owner = lax.rem(me - shift + bands, bands)
        y_ref[pl.ds(pl.multiple_of(owner * part, part), part), :] = ref[...]
    rows = lax.broadcasted_iota(jnp.int32, (members, members), 0)
    columns = lax.broadcasted_iota(jnp.int32, (members, members), 1)
    identity = (rows == columns).astype(F32)
    live = (lax.broadcasted_iota(jnp.int32, (1, slots), 1) < live_ref[0]).astype(F32)
    base = live * lax.rsqrt(variance_ref[...])
    scales, roots = [], []
    for g, point in enumerate(points):
        distance = (nearest_ref[...] - point).astype(F32)
        weight = jnp.exp(-0.25 * distance * distance) * base
        y = split2(y_ref[...] * weight)
        cross = dot_nt(y[0], y[1])
        cov = dot_nt(y[0], y[0]) + dot_nt(y[1], y[1]) + (cross + cross.T)
        cov = cov + (members - 1.0) * identity
        d0, d1 = split2(jnp.broadcast_to(weight * departure_ref[...], (8, slots)))
        right_ref[g] = dot_nt(d0, y[0]) + dot_nt(d0, y[1]) + dot_nt(d1, y[0])
        square_sum = jnp.sum(jnp.sum(cov * cov, axis=1, keepdims=True), axis=0, keepdims=True)
        scale = lax.rsqrt(square_sum)
        scales.append(scale)
        roots.append(cov * scale)
    count = len(points)
    us = quartics(roots, identity, mm1, mm1)
    for g in range(count):
        for i, piece in enumerate(split3(mm5(split3(roots[g]), us[g]))):
            root_ref[g, i] = piece
        inv_ref[g, 0], inv_ref[g, 1] = us[g]

    def products():
        return [
            mm3((inv_ref[g, 0], inv_ref[g, 1]), (root_ref[g, 0], root_ref[g, 1]))
            for g in range(count)
        ]

    def inverses(us):
        return [mm3(us[g], (inv_ref[g, 0], inv_ref[g, 1])) for g in range(count)]

    def step(square_mm, full):
        us = quartics(products(), identity, square_mm, mm1)
        if full:
            new = [
                mm5((root_ref[g, 0], root_ref[g, 1], root_ref[g, 2]), us[g])
                for g in range(count)
            ]
        else:
            new = [mm3((root_ref[g, 0], root_ref[g, 1]), us[g]) for g in range(count)]
        for g in range(count):
            pieces = split3(new[g]) if full else split2(new[g])
            for i, piece in enumerate(pieces):
                root_ref[g, i] = piece
        new = inverses(us)
        for g in range(count):
            inv_ref[g, 0], inv_ref[g, 1] = split2(new[g])

    def early(_, carry):
        step(mm1, True)
        return carry

    lax.fori_loop(0, NS_STEPS // 2 - 3, early, 0)
    step(mm3, False)
    lasts = inverses(quartics(products(), identity, mm3, mm3))
    for g in range(count):
        last = lasts[g]
        right = right_ref[g, 0:1, :]
        half = jnp.sum(last * right, axis=1, keepdims=True)
        mean_weights = jnp.sum(last * half, axis=0, keepdims=True) * scales[g]
        cov_ref[...] = last * jnp.sqrt((members - 1.0) * scales[g]) + mean_weights
        for shift in range(bands):
            target = lax.rem(me + shift, bands)
            rows = cov_ref[pl.ds(pl.multiple_of(target * part, part), part), :]
            if shift == 0:
                outs[0][g] = rows
            elif g < 2:
                outs[2 * shift - 1][g] = rows
            else:
                outs[2 * shift][g - 2] = rows


def solve(points, live, own, others, departure, variance, nearest):
    bands = 1 + len(others)
    part, slots = own.shape
    members = part * bands
    count = len(points)
    vmem = pl.BlockSpec(memory_space=pltpu.VMEM)
    return pl.pallas_call(
        functools.partial(solve_kernel, points, bands),
        out_shape=[jax.ShapeDtypeStruct((count, part, members), F32)]
        + [
            jax.ShapeDtypeStruct((n, part, members), F32)
            for _ in others
            for n in (2, count - 2)
        ],
        in_specs=[pl.BlockSpec(memory_space=pltpu.SMEM)] + [vmem] * (bands + 3),
        out_specs=[vmem] * (2 * bands - 1),
        scratch_shapes=[
            pltpu.VMEM((members, slots), F32),
            pltpu.VMEM((members, members), F32),
            pltpu.VMEM((count, 8, members), F32),
            pltpu.VMEM((count, 3, members, members), BF16),
            pltpu.VMEM((count, 2, members, members), BF16),
        ],
        compiler_params=pltpu.CompilerParams(vmem_limit_bytes=32 * MIB),
        cost_estimate=pl.CostEstimate(
            flops=2 * count * members * members * (3 * slots + 71 * members),
            bytes_accessed=4 * members * (slots + count * members),
            transcendentals=0,
        ),
        name="solve",
    )(live, own, *others, departure, variance, nearest)


def prepare_kernel(blocks, *refs):
    cells, (x_ref, mean_ref) = refs[:blocks], refs[blocks:]
    me = lax.axis_index("mem")
    members = x_ref.shape[3]
    strip = members // blocks
    total = sum(jnp.sum(ref[...], axis=2, keepdims=True) for ref in cells)
    mean = total * (1.0 / members)
    mean_ref[...] = jnp.broadcast_to(mean, mean_ref.shape)
    for shift, ref in enumerate(cells):
        x0, x1 = split2(ref[...] - mean)
        if blocks == 1:
            x_ref[0], x_ref[1] = x0, x1
        else:
            owner = lax.rem(me - shift + blocks, blocks)
            place = pl.ds(pl.multiple_of(owner * strip, strip), strip)
            x_ref[0, :, :, place] = x0
            x_ref[1, :, :, place] = x1


def prepare(cells, part):
    width, height, strip = cells[0].shape
    members = strip * len(cells)
    vmem = pl.BlockSpec(memory_space=pltpu.VMEM)
    return pl.pallas_call(
        functools.partial(prepare_kernel, len(cells)),
        out_shape=[
            jax.ShapeDtypeStruct((2, width, height, members), BF16),
            jax.ShapeDtypeStruct((width, height, part), F32),
        ],
        in_specs=[vmem] * len(cells),
        out_specs=[vmem] * 2,
        compiler_params=pltpu.CompilerParams(
            vmem_limit_bytes=16 * width * height * members + 8 * MIB
        ),
        cost_estimate=pl.CostEstimate(
            flops=8 * width * height * members,
            bytes_accessed=8 * width * height * members,
            transcendentals=0,
        ),
    )(*cells)


def column_intervals(width):
    spacing = width // CGX
    edges = [0] + [spacing * c + spacing // 2 for c in range(CGX)] + [width]
    return list(zip(edges[:-1], edges[1:]))


def window(refs, first):
    return [(ref, first - start) for ref, start in refs if start <= first][-1]


def add_terms(geometry, intervals, x_refs, t_ref, before_refs, out_refs, mine):
    width, height, bands = geometry
    part = out_refs[0][0].shape[2]
    members = x_refs[0][0].shape[3]
    spacing = width // CGX
    depth = height // bands
    for v in range(bands + 1):
        j0, j1 = max(depth * v - depth // 2, 0), min(depth * v + depth // 2, height)
        tall = j1 - j0
        j = lax.broadcasted_iota(jnp.int32, (1, tall, 1), 1).astype(F32) + (
            j0 + 0.5 - (v - 0.5) * depth
        )
        upper = j * (1.0 / depth)
        along_y = (1.0 - upper, upper)
        for c in intervals:
            i0, i1 = column_intervals(width)[c]
            wide = i1 - i0
            before, b0 = window(before_refs, i0)
            out, o0 = window(out_refs, i0)
            slots = [(v + a, c + b) for a in (0, 1) for b in (0, 1) if (v + a, c + b) in mine]
            result = before[b0 : b0 + wide, j0:j1, :]
            if slots:
                x, x_first = window(x_refs, i0)
                x0 = x[0, x_first : x_first + wide, j0:j1, :].reshape(wide * tall, members)
                x1 = x[1, x_first : x_first + wide, j0:j1, :].reshape(wide * tall, members)
                left = jnp.concatenate([x0, x0, x1], axis=1)
                i = lax.broadcasted_iota(jnp.int32, (wide, 1, 1), 0).astype(F32) + (
                    i0 + 0.5 - (c - 0.5) * spacing
                )
                right = i * (1.0 / spacing)
                along_x = (1.0 - right, right)
                t0 = jnp.concatenate([t_ref[mine[slot], 0] for slot in slots], axis=0)
                t1 = jnp.concatenate([t_ref[mine[slot], 1] for slot in slots], axis=0)
                product = dot_nt(left, jnp.concatenate([t0, t1, t0], axis=1))
                product = product.reshape(wide, tall, len(slots) * part)
                for n, (row, column) in enumerate(slots):
                    weight = along_x[column - c] * along_y[row - v]
                    result = result + weight * product[:, :, n * part : (n + 1) * part]
            out[o0 : o0 + wide, j0:j1, :] = result


def inner_slots(bands):
    names = [(row, column) for row in range(1, bands + 1) for column in range(1, CGX + 1)]
    return {name: n for n, name in enumerate(names)}


def edge_slots(bands):
    names = [(row, column) for row in (0, bands + 1) for column in (1, CGX)]
    names += [(row, column) for row in range(1, bands + 1) for column in (0, CGX + 1)]
    return {name: n for n, name in enumerate(names)}


def last_slots(bands):
    names = [(row, column) for row in (0, bands + 1) for column in range(2, CGX)]
    return {name: n for n, name in enumerate(names)}


def put(t_ref, slot, value):
    t0, t1 = split2(value)
    t_ref[slot, 0] = t0
    t_ref[slot, 1] = t1


def put_ends(t_ref, south, north, bands, tiles_y, shift, tile_value, end_value):
    me = lax.axis_index("mem")
    tile_y = lax.axis_index("gy")
    band = lax.rem(me - shift + bands, bands)

    @pl.when((tile_y == 0) & (band == 0))
    def _():
        put(t_ref, south, tile_value())

    @pl.when((tile_y == tiles_y - 1) & (band == bands - 1))
    def _():
        put(t_ref, north, tile_value())

    @pl.when((tile_y > 0) & (me == (shift - 1) % bands))
    def _():
        put(t_ref, south, end_value())

    @pl.when((tile_y < tiles_y - 1) & (me == shift))
    def _():
        put(t_ref, north, end_value())


def inner_kernel(geometry, intervals, first, *refs):
    bands = geometry[2]
    x_ref, mean_ref = refs[:2]
    rows = refs[2 : 2 * bands + 1]
    out_ref, t_ref = refs[2 * bands + 1 :]
    me = lax.axis_index("mem")
    for shift in range(bands):
        band = lax.rem(me - shift + bands, bands)
        for n, point in enumerate(POINTS):
            if point + 1 < intervals[0] or point > intervals[-1]:
                continue
            if shift == 0:
                value = rows[0][n]
            elif n < 2:
                value = rows[2 * shift - 1][n]
            else:
                value = rows[2 * shift][n - 2]
            put(t_ref, band * CGX + point, value)
    slots = inner_slots(bands)
    add_terms(
        geometry,
        intervals,
        [(x_ref, first)],
        t_ref,
        [(mean_ref, first)],
        [(out_ref, first)],
        slots,
    )


def edge_kernel(geometry, firsts, tiles_y, *refs):
    refs = list(refs)

    def take(n):
        taken, refs[:n] = refs[:n], []
        return taken

    bands = geometry[2]
    x_refs = list(zip(take(len(firsts)), firsts))
    before_refs = list(zip(take(len(firsts)), firsts))
    rows, ends, sides = take(bands), take(bands), take(2)
    out_ref, t_ref = refs
    me = lax.axis_index("mem")
    slots = edge_slots(bands)
    for shift in range(bands):
        band = lax.rem(me - shift + bands, bands)
        for n, point in enumerate(SIDES):
            put_ends(
                t_ref,
                slots[0, point + 1],
                slots[bands + 1, point + 1],
                bands,
                tiles_y,
                shift,
                lambda shift=shift, n=n: rows[shift][n],
                lambda shift=shift, n=n: ends[shift][n],
            )
        for side in (0, 1):
            put(t_ref, slots[1, 0] + 2 * band + side, sides[side][shift])
    add_terms(
        geometry, range(CGX + 1), x_refs, t_ref, before_refs, [(out_ref, 0)], slots
    )


def corner_kernel(bands, tiles_y, spacing, depth, *refs):
    edge_ref = refs[0]
    rows, ends = refs[1 : 1 + bands], refs[1 + bands : 1 + 2 * bands]
    left_ref, right_ref, t_ref = refs[1 + 2 * bands :]
    members = edge_ref.shape[3]
    part = left_ref.shape[2]
    for shift in range(bands):
        for n in (0, 1):
            put_ends(
                t_ref,
                n,
                2 + n,
                bands,
                tiles_y,
                shift,
                lambda shift=shift, n=n: rows[shift][n],
                lambda shift=shift, n=n: ends[shift][n],
            )
    half, tall = spacing // 2, depth // 2
    i = lax.broadcasted_iota(jnp.int32, (half, 1, 1), 0).astype(F32) + 0.5
    j = lax.broadcasted_iota(jnp.int32, (1, tall, 1), 1).astype(F32) + 0.5
    along_x = (i * (1.0 / spacing), 0.5 - i * (1.0 / spacing))
    along_y = (0.5 - j * (1.0 / depth), j * (1.0 / depth))
    for n, out_ref in enumerate((left_ref, right_ref)):
        for end in (0, 1):
            cells = slice(end * tall, (end + 1) * tall)
            first = 0 if n else half
            x0 = edge_ref[0, first : first + half, cells, :].reshape(half * tall, members)
            x1 = edge_ref[1, first : first + half, cells, :].reshape(half * tall, members)
            slot = 2 * end + n
            product = dot_nt(
                jnp.concatenate([x0, x0, x1], axis=1),
                jnp.concatenate([t_ref[slot, 0], t_ref[slot, 1], t_ref[slot, 0]], axis=1),
            )
            out_ref[:, cells, :] = (
                along_x[n] * along_y[end] * product.reshape(half, tall, part)
            )


def corners(bands, tiles_y, spacing, depth, edge, rows, ends):
    part, members = rows[0].shape[1:]
    vmem = pl.BlockSpec(memory_space=pltpu.VMEM)
    shape = jax.ShapeDtypeStruct((spacing // 2, depth, part), F32)
    return pl.pallas_call(
        functools.partial(corner_kernel, bands, tiles_y, spacing, depth),
        out_shape=[shape] * 2,
        in_specs=[vmem] * (1 + 2 * bands),
        out_specs=[vmem] * 2,
        scratch_shapes=[pltpu.VMEM((4, 2, part, members), BF16)],
        compiler_params=pltpu.CompilerParams(vmem_limit_bytes=16 * MIB),
        cost_estimate=pl.CostEstimate(
            flops=12 * spacing * depth * part * members,
            bytes_accessed=16 * part * members,
            transcendentals=0,
        ),
        name="corners",
    )(edge, *rows, *ends)


def last_kernel(geometry, firsts, tiles_y, *refs):
    refs = list(refs)

    def take(n):
        taken, refs[:n] = refs[:n], []
        return taken

    width, height, bands = geometry
    x_refs = list(zip(take(len(firsts)), firsts))
    (before_ref,) = take(1)
    rows, ends, given = take(bands), take(bands), take(2)
    out_ref, t_ref = refs
    slots = last_slots(bands)
    for shift in range(bands):
        for n in range(CGX - 2):
            k = 2 + n if shift == 0 else n
            put_ends(
                t_ref,
                slots[0, 2 + n],
                slots[bands + 1, 2 + n],
                bands,
                tiles_y,
                shift,
                lambda shift=shift, k=k: rows[shift][k],
                lambda shift=shift, k=k: ends[shift][k],
            )
    add_terms(
        geometry,
        range(CGX + 1),
        x_refs,
        t_ref,
        [(before_ref, 0)],
        [(out_ref, 0)],
        slots,
    )
    half, depth, _ = given[0].shape
    for ref, first in zip(given, (0, width - half)):
        for start, cells in ((0, 0), (depth // 2, height - depth // 2)):
            place = slice(cells, cells + depth // 2)
            out_ref[first : first + half, place, :] = (
                before_ref[first : first + half, place, :]
                + ref[:, start : start + depth // 2, :]
            )


def apply_terms(kernel, width, xs, befores, operands, slots, flops):
    _, _, height, members = xs[0].shape
    part = befores[0].shape[2]
    vmem = pl.BlockSpec(memory_space=pltpu.VMEM)
    operands = list(xs) + list(befores) + list(operands)
    size = sum(array.size * array.dtype.itemsize for array in operands)
    return pl.pallas_call(
        kernel,
        out_shape=jax.ShapeDtypeStruct((width, height, part), F32),
        in_specs=[vmem] * len(operands),
        out_specs=vmem,
        scratch_shapes=[pltpu.VMEM((len(slots), 2, part, members), BF16)],
        compiler_params=pltpu.CompilerParams(
            vmem_limit_bytes=min(size + 8 * width * height * part + 16 * MIB, 60 * MIB)
        ),
        cost_estimate=pl.CostEstimate(
            flops=flops, bytes_accessed=size, transcendentals=0
        ),
    )(*operands)


def shifted(array, axis, by):
    size = lax.axis_size(axis)
    return lax.ppermute(array, axis, [(i, (i + by) % size) for i in range(size)])


def to_next_tile(array, shift):
    bands = lax.axis_size("mem")
    tiles = lax.axis_size("gy")
    last, first = (shift - 1) % bands, shift
    pairs = [(last * tiles + y, last * tiles + y + 1) for y in range(tiles - 1)]
    pairs += [(first * tiles + y, first * tiles + y - 1) for y in range(1, tiles)]
    return lax.ppermute(array, ("mem", "gy"), pairs)


def analysis(background, anomalies, departure, variance, nearest, tally):
    bands = lax.axis_size("mem")
    tiles_y = lax.axis_size("gy")
    me = lax.axis_index("mem")
    part = background.shape[0]
    members = part * bands
    slots = departure.shape[3]

    def of_band(band):
        return lax.dynamic_slice_in_dim(anomalies, band * slots, slots, axis=3)

    others = [of_band(lax.rem(me + shift, bands)) for shift in range(1, bands)]
    anomalies, others = lax.optimization_barrier((anomalies, others))
    others = [shifted(piece.reshape(part, slots), "mem", s) for s, piece in enumerate(others, 1)]
    own = of_band(me).reshape(part, slots)
    tile = background.transpose(1, 2, 0)
    width, height = tile.shape[:2]
    spacing, depth = width // CGX, height // bands
    ends_y = jnp.concatenate([tile[:, : depth // 2], tile[:, height - depth // 2 :]], axis=1)
    edge = jnp.concatenate(
        [
            shifted(ends_y[: spacing // 2], "gx", -1),
            shifted(ends_y[width - spacing // 2 :], "gx", 1),
        ],
        axis=0,
    )

    def gathered(array):
        blocks = [array]
        for shift in range(1, bands):
            blocks.append(shifted(array, "mem", shift))
        if part % 128:
            order = lax.rem(me - jnp.arange(bands) + bands, bands)
            blocks = jnp.take(jnp.stack(blocks, axis=2), order, axis=2)
            blocks = [blocks.reshape(blocks.shape[:2] + (members,))]
        return blocks

    firsts = (0, column_intervals(width)[CGX - 1][0])
    cells = [gathered(tile[: firsts[1]]), gathered(tile[firsts[1] :])]
    edges = gathered(edge)
    solved = solve(
        POINTS,
        tally.reshape(1),
        own,
        others,
        departure.reshape(1, slots),
        variance.reshape(1, slots),
        nearest.reshape(1, slots),
    )
    row = solved[0]
    other_side = [shifted(solved[2 * s - 1], "mem", s) for s in range(1, bands)]
    other_mid = [shifted(solved[2 * s], "mem", s) for s in range(1, bands)]
    own_end = to_next_tile(row, 0)
    ends_side = [to_next_tile(other_side[s - 1], s) for s in range(1, bands)]
    row_sides = [
        shifted(jnp.stack([row[n]] + [array[n] for array in other_side]), "gx", by)
        for n, by in ((1, 1), (0, -1))
    ]
    ends_mid = [to_next_tile(other_mid[s - 1], s) for s in range(1, bands)]
    geometry = (width, height, bands)
    edge, _ = prepare(edges, part)
    x_first, mean_first = prepare(cells[0], part)
    left, right = corners(
        bands, tiles_y, spacing, depth, edge, [row] + other_side, [own_end] + ends_side
    )
    given = [shifted(right, "gx", 1), shifted(left, "gx", -1)]
    operands = [row]
    for side, mid in zip(other_side, other_mid):
        operands += [side, mid]
    work = 6 * width * height * part * members

    def inner(x, mean, intervals, first):
        return apply_terms(
            functools.partial(inner_kernel, geometry, intervals, first),
            x.shape[1],
            [x],
            [mean],
            operands,
            inner_slots(bands),
            3 * work * x.shape[1] // width,
        )

    inner_first = inner(x_first, mean_first, range(CGX - 1), 0)
    x_second, mean_second = prepare(cells[1], part)
    inner_second = inner(x_second, mean_second, range(CGX - 1, CGX + 1), firsts[1])
    xs = [x_first, x_second]
    result = apply_terms(
        functools.partial(edge_kernel, geometry, firsts, tiles_y),
        width,
        xs,
        [inner_first, inner_second],
        [row] + other_side + [own_end] + ends_side + row_sides,
        edge_slots(bands),
        work,
    )
    result = apply_terms(
        functools.partial(last_kernel, geometry, firsts, tiles_y),
        width,
        xs,
        [result],
        [row] + other_mid + [own_end] + ends_mid + given,
        last_slots(bands),
        work // 2,
    )
    return result.transpose(2, 0, 1)


def solution(mesh):
    in_specs = (
        P("mem", "gx", "gy"),
        P("mem", "gx", "gy", None),
        P("gx", "gy", "mem", None),
        P("gx", "gy", "mem", None),
        P("gx", "gy", "mem", None),
        P("gx", "gy", "mem"),
    )
    out_specs = P("mem", "gx", "gy")
    return jax.shard_map(
        analysis, mesh=mesh, in_specs=in_specs, out_specs=out_specs, check_vma=False
    )
```

```python
import functools

import jax
import jax.numpy as jnp
from jax import lax
from jax.experimental import pallas as pl
from jax.experimental.pallas import tpu as pltpu
from jax.sharding import PartitionSpec as P


CGX = 4
NS_STEPS = 12
SIDES = (0, CGX - 1)
POINTS = SIDES + tuple(range(1, CGX - 1))

F32 = jnp.float32
BF16 = jnp.bfloat16
MIB = 1024 * 1024
NT = (((1,), (1,)), ((), ()))


def dot(a, b):
    return jnp.dot(a, b, preferred_element_type=F32)


def dot_nt(a, b):
    return lax.dot_general(a, b, NT, preferred_element_type=F32)


def split2(x):
    high = x.astype(BF16)
    return high, (x - high.astype(F32)).astype(BF16)


def split3(x):
    high = x.astype(BF16)
    rest = x - high.astype(F32)
    mid = rest.astype(BF16)
    return high, mid, (rest - mid.astype(F32)).astype(BF16)


def mm3(a, b):
    return dot(
        jnp.concatenate([a[0], a[0], a[1]], axis=1),
        jnp.concatenate([b[0], b[1], b[0]], axis=0),
    )


def mm5(a, b):
    return dot(
        jnp.concatenate([a[0], a[1], a[2], a[0], a[1]], axis=1),
        jnp.concatenate([b[0], b[0], b[0], b[1], b[1]], axis=0),
    )


def mm1(a, b):
    return dot(a[0], b[0])


def quartics(ps, identity, square_mm, inner_mm):
    squares = [square_mm(piece, piece) for piece in [split2(p) for p in ps]]
    inner = [
        inner_mm(split2(square), split2(0.0625 * square - 0.5625 * p))
        for p, square in zip(ps, squares)
    ]
    return [
        split2(product + (1.6875 * square + (2.25 * identity - 2.4375 * p)))
        for p, square, product in zip(ps, squares, inner)
    ]


def solve_kernel(points, bands, live_ref, own_ref, *refs):
    others = refs[: bands - 1]
    departure_ref, variance_ref, nearest_ref = refs[bands - 1 : bands + 2]
    outs = refs[bands + 2 : 3 * bands + 1]
    y_ref, cov_ref, right_ref, root_ref, inv_ref = refs[3 * bands + 1 :]
    me = lax.axis_index("mem")
    part, slots = own_ref.shape
    members = y_ref.shape[0]
    for shift, ref in enumerate((own_ref,) + tuple(others)):
        owner = lax.rem(me - shift + bands, bands)
        y_ref[pl.ds(pl.multiple_of(owner * part, part), part), :] = ref[...]
    rows = lax.broadcasted_iota(jnp.int32, (members, members), 0)
    columns = lax.broadcasted_iota(jnp.int32, (members, members), 1)
    identity = (rows == columns).astype(F32)
    live = (lax.broadcasted_iota(jnp.int32, (1, slots), 1) < live_ref[0]).astype(F32)
    base = live * lax.rsqrt(variance_ref[...])
    scales, roots = [], []
    for g, point in enumerate(points):
        distance = (nearest_ref[...] - point).astype(F32)
        weight = jnp.exp(-0.25 * distance * distance) * base
        y = split2(y_ref[...] * weight)
        cross = dot_nt(y[0], y[1])
        cov = dot_nt(y[0], y[0]) + dot_nt(y[1], y[1]) + (cross + cross.T)
        cov = cov + (members - 1.0) * identity
        d0, d1 = split2(jnp.broadcast_to(weight * departure_ref[...], (8, slots)))
        right_ref[g] = dot_nt(d0, y[0]) + dot_nt(d0, y[1]) + dot_nt(d1, y[0])
        square_sum = jnp.sum(jnp.sum(cov * cov, axis=1, keepdims=True), axis=0, keepdims=True)
        scale = lax.rsqrt(square_sum)
        scales.append(scale)
        roots.append(cov * scale)
    count = len(points)
    us = quartics(roots, identity, mm1, mm1)
    for g in range(count):
        for i, piece in enumerate(split3(mm5(split3(roots[g]), us[g]))):
            root_ref[g, i] = piece
        inv_ref[g, 0], inv_ref[g, 1] = us[g]

    def products():
        return [
            mm3((inv_ref[g, 0], inv_ref[g, 1]), (root_ref[g, 0], root_ref[g, 1]))
            for g in range(count)
        ]

    def inverses(us):
        return [mm3(us[g], (inv_ref[g, 0], inv_ref[g, 1])) for g in range(count)]

    def step(square_mm, full):
        us = quartics(products(), identity, square_mm, mm1)
        if full:
            new = [
                mm5((root_ref[g, 0], root_ref[g, 1], root_ref[g, 2]), us[g])
                for g in range(count)
            ]
        else:
            new = [mm3((root_ref[g, 0], root_ref[g, 1]), us[g]) for g in range(count)]
        for g in range(count):
            pieces = split3(new[g]) if full else split2(new[g])
            for i, piece in enumerate(pieces):
                root_ref[g, i] = piece
        new = inverses(us)
        for g in range(count):
            inv_ref[g, 0], inv_ref[g, 1] = split2(new[g])

    def early(_, carry):
        step(mm1, True)
        return carry

    lax.fori_loop(0, NS_STEPS // 2 - 3, early, 0)
    step(mm3, False)
    lasts = inverses(quartics(products(), identity, mm3, mm3))
    for g in range(count):
        last = lasts[g]
        right = right_ref[g, 0:1, :]
        half = jnp.sum(last * right, axis=1, keepdims=True)
        mean_weights = jnp.sum(last * half, axis=0, keepdims=True) * scales[g]
        cov_ref[...] = last * jnp.sqrt((members - 1.0) * scales[g]) + mean_weights
        for shift in range(bands):
            target = lax.rem(me + shift, bands)
            rows = cov_ref[pl.ds(pl.multiple_of(target * part, part), part), :]
            if shift == 0:
                outs[0][g] = rows
            elif g < 2:
                outs[2 * shift - 1][g] = rows
            else:
                outs[2 * shift][g - 2] = rows


def solve(points, live, own, others, departure, variance, nearest):
    bands = 1 + len(others)
    part, slots = own.shape
    members = part * bands
    count = len(points)
    vmem = pl.BlockSpec(memory_space=pltpu.VMEM)
    return pl.pallas_call(
        functools.partial(solve_kernel, points, bands),
        out_shape=[jax.ShapeDtypeStruct((count, part, members), F32)]
        + [
            jax.ShapeDtypeStruct((n, part, members), F32)
            for _ in others
            for n in (2, count - 2)
        ],
        in_specs=[pl.BlockSpec(memory_space=pltpu.SMEM)] + [vmem] * (bands + 3),
        out_specs=[vmem] * (2 * bands - 1),
        scratch_shapes=[
            pltpu.VMEM((members, slots), F32),
            pltpu.VMEM((members, members), F32),
            pltpu.VMEM((count, 8, members), F32),
            pltpu.VMEM((count, 3, members, members), BF16),
            pltpu.VMEM((count, 2, members, members), BF16),
        ],
        compiler_params=pltpu.CompilerParams(vmem_limit_bytes=32 * MIB),
        cost_estimate=pl.CostEstimate(
            flops=2 * count * members * members * (3 * slots + 71 * members),
            bytes_accessed=4 * members * (slots + count * members),
            transcendentals=0,
        ),
        name="solve",
    )(live, own, *others, departure, variance, nearest)


def prepare_kernel(blocks, *refs):
    cells, (x_ref, mean_ref) = refs[:blocks], refs[blocks:]
    me = lax.axis_index("mem")
    members = x_ref.shape[3]
    strip = members // blocks
    total = sum(jnp.sum(ref[...], axis=2, keepdims=True) for ref in cells)
    mean = total * (1.0 / members)
    mean_ref[...] = jnp.broadcast_to(mean, mean_ref.shape)
    for shift, ref in enumerate(cells):
        x0, x1 = split2(ref[...] - mean)
        if blocks == 1:
            x_ref[0], x_ref[1] = x0, x1
        else:
            owner = lax.rem(me - shift + blocks, blocks)
            place = pl.ds(pl.multiple_of(owner * strip, strip), strip)
            x_ref[0, :, :, place] = x0
            x_ref[1, :, :, place] = x1


def prepare(cells, part):
    width, height, strip = cells[0].shape
    members = strip * len(cells)
    vmem = pl.BlockSpec(memory_space=pltpu.VMEM)
    return pl.pallas_call(
        functools.partial(prepare_kernel, len(cells)),
        out_shape=[
            jax.ShapeDtypeStruct((2, width, height, members), BF16),
            jax.ShapeDtypeStruct((width, height, part), F32),
        ],
        in_specs=[vmem] * len(cells),
        out_specs=[vmem] * 2,
        compiler_params=pltpu.CompilerParams(
            vmem_limit_bytes=16 * width * height * members + 8 * MIB
        ),
        cost_estimate=pl.CostEstimate(
            flops=8 * width * height * members,
            bytes_accessed=8 * width * height * members,
            transcendentals=0,
        ),
    )(*cells)


def column_intervals(width):
    spacing = width // CGX
    edges = [0] + [spacing * c + spacing // 2 for c in range(CGX)] + [width]
    return list(zip(edges[:-1], edges[1:]))


def window(refs, first):
    return [(ref, first - start) for ref, start in refs if start <= first][-1]


def add_terms(geometry, intervals, x_refs, t_ref, before_refs, out_refs, mine):
    width, height, bands = geometry
    part = out_refs[0][0].shape[2]
    members = x_refs[0][0].shape[3]
    spacing = width // CGX
    depth = height // bands
    for v in range(bands + 1):
        j0, j1 = max(depth * v - depth // 2, 0), min(depth * v + depth // 2, height)
        tall = j1 - j0
        j = lax.broadcasted_iota(jnp.int32, (1, tall, 1), 1).astype(F32) + (
            j0 + 0.5 - (v - 0.5) * depth
        )
        upper = j * (1.0 / depth)
        along_y = (1.0 - upper, upper)
        for c in intervals:
            i0, i1 = column_intervals(width)[c]
            wide = i1 - i0
            before, b0 = window(before_refs, i0)
            out, o0 = window(out_refs, i0)
            slots = [(v + a, c + b) for a in (0, 1) for b in (0, 1) if (v + a, c + b) in mine]
            result = before[b0 : b0 + wide, j0:j1, :]
            if slots:
                x, x_first = window(x_refs, i0)
                x0 = x[0, x_first : x_first + wide, j0:j1, :].reshape(wide * tall, members)
                x1 = x[1, x_first : x_first + wide, j0:j1, :].reshape(wide * tall, members)
                left = jnp.concatenate([x0, x0, x1], axis=1)
                i = lax.broadcasted_iota(jnp.int32, (wide, 1, 1), 0).astype(F32) + (
                    i0 + 0.5 - (c - 0.5) * spacing
                )
                right = i * (1.0 / spacing)
                along_x = (1.0 - right, right)
                t0 = jnp.concatenate([t_ref[mine[slot], 0] for slot in slots], axis=0)
                t1 = jnp.concatenate([t_ref[mine[slot], 1] for slot in slots], axis=0)
                product = dot_nt(left, jnp.concatenate([t0, t1, t0], axis=1))
                product = product.reshape(wide, tall, len(slots) * part)
                for n, (row, column) in enumerate(slots):
                    weight = along_x[column - c] * along_y[row - v]
                    result = result + weight * product[:, :, n * part : (n + 1) * part]
            out[o0 : o0 + wide, j0:j1, :] = result


def inner_slots(bands):
    names = [(row, column) for row in range(1, bands + 1) for column in range(1, CGX + 1)]
    return {name: n for n, name in enumerate(names)}


def all_slots(bands):
    names = [(row, column) for row in range(bands + 2) for column in range(CGX + 2)]
    return {name: n for n, name in enumerate(names)}


def put(t_ref, slot, value):
    t0, t1 = split2(value)
    t_ref[slot, 0] = t0
    t_ref[slot, 1] = t1


def put_ends(t_ref, south, north, bands, tiles_y, shift, tile_value, end_value):
    me = lax.axis_index("mem")
    tile_y = lax.axis_index("gy")
    band = lax.rem(me - shift + bands, bands)

    @pl.when((tile_y == 0) & (band == 0))
    def _():
        put(t_ref, south, tile_value())

    @pl.when((tile_y == tiles_y - 1) & (band == bands - 1))
    def _():
        put(t_ref, north, tile_value())

    @pl.when((tile_y > 0) & (me == (shift - 1) % bands))
    def _():
        put(t_ref, south, end_value())

    @pl.when((tile_y < tiles_y - 1) & (me == shift))
    def _():
        put(t_ref, north, end_value())


def inner_kernel(geometry, intervals, first, *refs):
    bands = geometry[2]
    x_ref, mean_ref = refs[:2]
    rows = refs[2 : 2 * bands + 1]
    out_ref, t_ref = refs[2 * bands + 1 :]
    me = lax.axis_index("mem")
    for shift in range(bands):
        band = lax.rem(me - shift + bands, bands)
        for n, point in enumerate(POINTS):
            if point + 1 < intervals[0] or point > intervals[-1]:
                continue
            if shift == 0:
                value = rows[0][n]
            elif n < 2:
                value = rows[2 * shift - 1][n]
            else:
                value = rows[2 * shift][n - 2]
            put(t_ref, band * CGX + point, value)
    slots = inner_slots(bands)
    add_terms(
        geometry,
        intervals,
        [(x_ref, first)],
        t_ref,
        [(mean_ref, first)],
        [(out_ref, first)],
        slots,
    )


def corner_kernel(bands, tiles_y, spacing, depth, *refs):
    edge_ref = refs[0]
    rows, ends = refs[1 : 1 + bands], refs[1 + bands : 1 + 2 * bands]
    left_ref, right_ref, t_ref = refs[1 + 2 * bands :]
    members = edge_ref.shape[3]
    part = left_ref.shape[2]
    for shift in range(bands):
        for n in (0, 1):
            put_ends(
                t_ref,
                n,
                2 + n,
                bands,
                tiles_y,
                shift,
                lambda shift=shift, n=n: rows[shift][n],
                lambda shift=shift, n=n: ends[shift][n],
            )
    half, tall = spacing // 2, depth // 2
    i = lax.broadcasted_iota(jnp.int32, (half, 1, 1), 0).astype(F32) + 0.5
    j = lax.broadcasted_iota(jnp.int32, (1, tall, 1), 1).astype(F32) + 0.5
    along_x = (i * (1.0 / spacing), 0.5 - i * (1.0 / spacing))
    along_y = (0.5 - j * (1.0 / depth), j * (1.0 / depth))
    for n, out_ref in enumerate((left_ref, right_ref)):
        for end in (0, 1):
            cells = slice(end * tall, (end + 1) * tall)
            first = 0 if n else half
            x0 = edge_ref[0, first : first + half, cells, :].reshape(half * tall, members)
            x1 = edge_ref[1, first : first + half, cells, :].reshape(half * tall, members)
            slot = 2 * end + n
            product = dot_nt(
                jnp.concatenate([x0, x0, x1], axis=1),
                jnp.concatenate([t_ref[slot, 0], t_ref[slot, 1], t_ref[slot, 0]], axis=1),
            )
            out_ref[:, cells, :] = (
                along_x[n] * along_y[end] * product.reshape(half, tall, part)
            )


def corners(bands, tiles_y, spacing, depth, edge, rows, ends):
    part, members = rows[0].shape[1:]
    vmem = pl.BlockSpec(memory_space=pltpu.VMEM)
    shape = jax.ShapeDtypeStruct((spacing // 2, depth, part), F32)
    return pl.pallas_call(
        functools.partial(corner_kernel, bands, tiles_y, spacing, depth),
        out_shape=[shape] * 2,
        in_specs=[vmem] * (1 + 2 * bands),
        out_specs=[vmem] * 2,
        scratch_shapes=[pltpu.VMEM((4, 2, part, members), BF16)],
        compiler_params=pltpu.CompilerParams(vmem_limit_bytes=16 * MIB),
        cost_estimate=pl.CostEstimate(
            flops=12 * spacing * depth * part * members,
            bytes_accessed=16 * part * members,
            transcendentals=0,
        ),
        name="corners",
    )(edge, *rows, *ends)


def final_kernel(geometry, firsts, tiles_y, *refs):
    refs = list(refs)

    def take(n):
        taken, refs[:n] = refs[:n], []
        return taken

    width, height, bands = geometry
    x_refs = list(zip(take(2), firsts))
    before_refs = list(zip(take(2), firsts))
    row, own_end = take(2)
    other_side, other_mid = take(bands - 1), take(bands - 1)
    ends_side, ends_mid = take(bands - 1), take(bands - 1)
    sides, given = take(2), take(2)
    out_ref, t_ref = refs
    me = lax.axis_index("mem")
    slots = all_slots(bands)
    for shift in range(bands):
        band = lax.rem(me - shift + bands, bands)
        for n, point in enumerate(POINTS):
            if shift == 0:
                here, there, k = row, own_end, n
            elif n < 2:
                here, there, k = other_side[shift - 1], ends_side[shift - 1], n
            else:
                here, there, k = other_mid[shift - 1], ends_mid[shift - 1], n - 2
            if point + 2 >= CGX:
                put(t_ref, (band + 1) * (CGX + 2) + point + 1, here[k])
            put_ends(
                t_ref,
                slots[0, point + 1],
                slots[bands + 1, point + 1],
                bands,
                tiles_y,
                shift,
                lambda here=here, k=k: here[k],
                lambda there=there, k=k: there[k],
            )
        for side, column in enumerate((0, CGX + 1)):
            put(t_ref, (band + 1) * (CGX + 2) + column, sides[side][shift])
    rows, columns = range(1, bands + 1), range(1, CGX + 1)
    late = {s: n for s, n in slots.items() if (s[0] in rows) != (s[1] in columns)}
    both = {s: n for s, n in slots.items() if s[0] in rows or s[1] in columns}
    for intervals, mine in ((range(CGX - 1), late), (range(CGX - 1, CGX + 1), both)):
        add_terms(
            geometry, intervals, x_refs, t_ref, before_refs, [(out_ref, 0)], mine
        )
    half, depth, _ = given[0].shape
    for ref, first in zip(given, (0, width - half)):
        for start, cells in ((0, 0), (depth // 2, height - depth // 2)):
            place = slice(cells, cells + depth // 2)
            out_ref[first : first + half, place, :] += ref[:, start : start + depth // 2, :]


def apply_terms(kernel, width, xs, befores, operands, slots, flops):
    _, _, height, members = xs[0].shape
    part = befores[0].shape[2]
    vmem = pl.BlockSpec(memory_space=pltpu.VMEM)
    operands = list(xs) + list(befores) + list(operands)
    size = sum(array.size * array.dtype.itemsize for array in operands)
    return pl.pallas_call(
        kernel,
        out_shape=jax.ShapeDtypeStruct((width, height, part), F32),
        in_specs=[vmem] * len(operands),
        out_specs=vmem,
        scratch_shapes=[pltpu.VMEM((len(slots), 2, part, members), BF16)],
        compiler_params=pltpu.CompilerParams(
            vmem_limit_bytes=min(size + 8 * width * height * part + 16 * MIB, 60 * MIB)
        ),
        cost_estimate=pl.CostEstimate(
            flops=flops, bytes_accessed=size, transcendentals=0
        ),
    )(*operands)


def shifted(array, axis, by):
    size = lax.axis_size(axis)
    return lax.ppermute(array, axis, [(i, (i + by) % size) for i in range(size)])


def to_next_tile(array, shift):
    bands = lax.axis_size("mem")
    tiles = lax.axis_size("gy")
    last, first = (shift - 1) % bands, shift
    pairs = [(last * tiles + y, last * tiles + y + 1) for y in range(tiles - 1)]
    pairs += [(first * tiles + y, first * tiles + y - 1) for y in range(1, tiles)]
    return lax.ppermute(array, ("mem", "gy"), pairs)


def analysis(background, anomalies, departure, variance, nearest, tally):
    bands = lax.axis_size("mem")
    tiles_y = lax.axis_size("gy")
    me = lax.axis_index("mem")
    part = background.shape[0]
    members = part * bands
    slots = departure.shape[3]

    def of_band(band):
        return lax.dynamic_slice_in_dim(anomalies, band * slots, slots, axis=3)

    others = [of_band(lax.rem(me + shift, bands)) for shift in range(1, bands)]
    anomalies, others = lax.optimization_barrier((anomalies, others))
    others = [shifted(piece.reshape(part, slots), "mem", s) for s, piece in enumerate(others, 1)]
    own = of_band(me).reshape(part, slots)
    tile = background.transpose(1, 2, 0)
    width, height = tile.shape[:2]
    spacing, depth = width // CGX, height // bands
    ends_y = jnp.concatenate([tile[:, : depth // 2], tile[:, height - depth // 2 :]], axis=1)
    edge = jnp.concatenate(
        [
            shifted(ends_y[: spacing // 2], "gx", -1),
            shifted(ends_y[width - spacing // 2 :], "gx", 1),
        ],
        axis=0,
    )

    def gathered(array):
        blocks = [array]
        for shift in range(1, bands):
            blocks.append(shifted(array, "mem", shift))
        if part % 128:
            order = lax.rem(me - jnp.arange(bands) + bands, bands)
            blocks = jnp.take(jnp.stack(blocks, axis=2), order, axis=2)
            blocks = [blocks.reshape(blocks.shape[:2] + (members,))]
        return blocks

    firsts = (0, column_intervals(width)[CGX - 1][0])
    tally, second = lax.optimization_barrier((tally, tile[firsts[1] :]))
    cells = [gathered(tile[: firsts[1]]), gathered(second)]
    edges = gathered(edge)
    solved = solve(
        POINTS,
        tally.reshape(1),
        own,
        others,
        departure.reshape(1, slots),
        variance.reshape(1, slots),
        nearest.reshape(1, slots),
    )
    row = solved[0]
    other_side = [shifted(solved[2 * s - 1], "mem", s) for s in range(1, bands)]
    other_mid = [shifted(solved[2 * s], "mem", s) for s in range(1, bands)]
    own_end = to_next_tile(row, 0)
    ends_side = [to_next_tile(other_side[s - 1], s) for s in range(1, bands)]
    row_sides = [
        shifted(jnp.stack([row[n]] + [array[n] for array in other_side]), "gx", by)
        for n, by in ((1, 1), (0, -1))
    ]
    ends_mid = [to_next_tile(other_mid[s - 1], s) for s in range(1, bands)]
    geometry = (width, height, bands)
    edge, _ = prepare(edges, part)
    x_first, mean_first = prepare(cells[0], part)
    left, right = corners(
        bands, tiles_y, spacing, depth, edge, [row] + other_side, [own_end] + ends_side
    )
    given = [shifted(right, "gx", 1), shifted(left, "gx", -1)]
    operands = [row]
    for side, mid in zip(other_side, other_mid):
        operands += [side, mid]
    work = 6 * width * height * part * members

    inner_first = apply_terms(
        functools.partial(inner_kernel, geometry, range(CGX - 1), 0),
        firsts[1],
        [x_first],
        [mean_first],
        operands,
        inner_slots(bands),
        work,
    )
    x_second, mean_second = prepare(cells[1], part)
    result = apply_terms(
        functools.partial(final_kernel, geometry, firsts, tiles_y),
        width,
        [x_first, x_second],
        [inner_first, mean_second],
        [row, own_end]
        + other_side
        + other_mid
        + ends_side
        + ends_mid
        + row_sides
        + given,
        all_slots(bands),
        2 * work,
    )
    return result.transpose(2, 0, 1)


def solution(mesh):
    in_specs = (
        P("mem", "gx", "gy"),
        P("mem", "gx", "gy", None),
        P("gx", "gy", "mem", None),
        P("gx", "gy", "mem", None),
        P("gx", "gy", "mem", None),
        P("gx", "gy", "mem"),
    )
    out_specs = P("mem", "gx", "gy")
    return jax.shard_map(
        analysis, mesh=mesh, in_specs=in_specs, out_specs=out_specs, check_vma=False
    )
```

```python
import functools

import jax
import jax.numpy as jnp
from jax import lax
from jax.experimental import pallas as pl
from jax.experimental.pallas import tpu as pltpu
from jax.sharding import PartitionSpec as P


CGX = 4
NS_STEPS = 12
SIDES = (0, CGX - 1)
POINTS = SIDES + tuple(range(1, CGX - 1))

F32 = jnp.float32
BF16 = jnp.bfloat16
MIB = 1024 * 1024
NT = (((1,), (1,)), ((), ()))


def dot(a, b):
    return jnp.dot(a, b, preferred_element_type=F32)


def dot_nt(a, b):
    return lax.dot_general(a, b, NT, preferred_element_type=F32)


def split2(x):
    high = x.astype(BF16)
    return high, (x - high.astype(F32)).astype(BF16)


def split3(x):
    high = x.astype(BF16)
    rest = x - high.astype(F32)
    mid = rest.astype(BF16)
    return high, mid, (rest - mid.astype(F32)).astype(BF16)


def mm3(a, b):
    return dot(
        jnp.concatenate([a[0], a[0], a[1]], axis=1),
        jnp.concatenate([b[0], b[1], b[0]], axis=0),
    )


def mm5(a, b):
    return dot(
        jnp.concatenate([a[0], a[1], a[2], a[0], a[1]], axis=1),
        jnp.concatenate([b[0], b[0], b[0], b[1], b[1]], axis=0),
    )


def mm1(a, b):
    return dot(a[0], b[0])


def quartics(ps, identity, square_mm, inner_mm):
    squares = [square_mm(piece, piece) for piece in [split2(p) for p in ps]]
    inner = [
        inner_mm(split2(square), split2(0.0625 * square - 0.5625 * p))
        for p, square in zip(ps, squares)
    ]
    return [
        split2(product + (1.6875 * square + (2.25 * identity - 2.4375 * p)))
        for p, square, product in zip(ps, squares, inner)
    ]


def solve_kernel(points, bands, live_ref, own_ref, *refs):
    others = refs[: bands - 1]
    departure_ref, variance_ref, nearest_ref = refs[bands - 1 : bands + 2]
    outs = refs[bands + 2 : 3 * bands + 1]
    y_ref, z_ref, cov_ref, right_ref, root_ref, inv_ref = refs[3 * bands + 1 :]
    me = lax.axis_index("mem")
    part, slots = own_ref.shape
    members = y_ref.shape[0]
    for shift, ref in enumerate((own_ref,) + tuple(others)):
        owner = lax.rem(me - shift + bands, bands)
        y_ref[pl.ds(pl.multiple_of(owner * part, part), part), :] = ref[...]
    rows = lax.broadcasted_iota(jnp.int32, (members, members), 0)
    columns = lax.broadcasted_iota(jnp.int32, (members, members), 1)
    identity = (rows == columns).astype(F32)
    live = (lax.broadcasted_iota(jnp.int32, (1, slots), 1) < live_ref[0]).astype(F32)
    base = live * lax.rsqrt(variance_ref[...])
    scales, roots, sums = [], [], []
    count = len(points)

    def split(g):
        distance = (nearest_ref[...] - points[g]).astype(F32)
        weight = jnp.exp(-0.25 * distance * distance) * base
        y0, y1 = split2(y_ref[...] * weight)
        d0, d1 = split2(weight * departure_ref[...])
        z_ref[g, :members], z_ref[g, members : 2 * members] = y0, y1
        z_ref[g, 2 * members :] = jnp.concatenate(
            [jnp.broadcast_to(d0, (16, slots)), jnp.broadcast_to(d1, (16, slots))], axis=0
        )

    split(0)
    for g in range(count):
        first = dot_nt(z_ref[g], z_ref[g, :members])
        if g + 1 < count:
            split(g + 1)
        second = dot_nt(z_ref[g, members : 2 * members + 16], z_ref[g, members : 2 * members])
        sums.append((first, second))
    for first, second in sums:
        cross = first[members : 2 * members]
        cov = first[:members] + second[:members] + (cross + cross.T)
        cov = cov + (members - 1.0) * identity
        right = first[2 * members :]
        right_ref[len(roots)] = right[:8] + right[16:24] + second[members : members + 8]
        square_sum = jnp.sum(jnp.sum(cov * cov, axis=1, keepdims=True), axis=0, keepdims=True)
        scale = lax.rsqrt(square_sum)
        scales.append(scale)
        roots.append(cov * scale)
    us = quartics(roots, identity, mm1, mm1)
    for g in range(count):
        for i, piece in enumerate(split3(mm5(split3(roots[g]), us[g]))):
            root_ref[g, i] = piece
        inv_ref[g, 0], inv_ref[g, 1] = us[g]

    def products():
        return [
            mm3((inv_ref[g, 0], inv_ref[g, 1]), (root_ref[g, 0], root_ref[g, 1]))
            for g in range(count)
        ]

    def inverses(us):
        return [mm3(us[g], (inv_ref[g, 0], inv_ref[g, 1])) for g in range(count)]

    def step(square_mm, full):
        us = quartics(products(), identity, square_mm, mm1)
        if full:
            new = [
                mm5((root_ref[g, 0], root_ref[g, 1], root_ref[g, 2]), us[g])
                for g in range(count)
            ]
        else:
            new = [mm3((root_ref[g, 0], root_ref[g, 1]), us[g]) for g in range(count)]
        for g in range(count):
            pieces = split3(new[g]) if full else split2(new[g])
            for i, piece in enumerate(pieces):
                root_ref[g, i] = piece
        new = inverses(us)
        for g in range(count):
            inv_ref[g, 0], inv_ref[g, 1] = split2(new[g])

    def early(_, carry):
        step(mm1, True)
        return carry

    lax.fori_loop(0, NS_STEPS // 2 - 3, early, 0)
    step(mm3, False)
    lasts = inverses(quartics(products(), identity, mm3, mm3))
    for g in range(count):
        last = lasts[g]
        right = right_ref[g, 0:1, :]
        half = jnp.sum(last * right, axis=1, keepdims=True)
        mean_weights = jnp.sum(last * half, axis=0, keepdims=True) * scales[g]
        cov_ref[...] = last * jnp.sqrt((members - 1.0) * scales[g]) + mean_weights
        for shift in range(bands):
            target = lax.rem(me + shift, bands)
            rows = cov_ref[pl.ds(pl.multiple_of(target * part, part), part), :]
            if shift == 0:
                outs[0][g] = rows
            elif g < 2:
                outs[2 * shift - 1][g] = rows
            else:
                outs[2 * shift][g - 2] = rows


def solve(points, live, own, others, departure, variance, nearest):
    bands = 1 + len(others)
    part, slots = own.shape
    members = part * bands
    count = len(points)
    vmem = pl.BlockSpec(memory_space=pltpu.VMEM)
    return pl.pallas_call(
        functools.partial(solve_kernel, points, bands),
        out_shape=[jax.ShapeDtypeStruct((count, part, members), F32)]
        + [
            jax.ShapeDtypeStruct((n, part, members), F32)
            for _ in others
            for n in (2, count - 2)
        ],
        in_specs=[pl.BlockSpec(memory_space=pltpu.SMEM)] + [vmem] * (bands + 3),
        out_specs=[vmem] * (2 * bands - 1),
        scratch_shapes=[
            pltpu.VMEM((members, slots), F32),
            pltpu.VMEM((count, 2 * members + 32, slots), BF16),
            pltpu.VMEM((members, members), F32),
            pltpu.VMEM((count, 8, members), F32),
            pltpu.VMEM((count, 3, members, members), BF16),
            pltpu.VMEM((count, 2, members, members), BF16),
        ],
        compiler_params=pltpu.CompilerParams(vmem_limit_bytes=32 * MIB),
        cost_estimate=pl.CostEstimate(
            flops=2 * count * members * members * (3 * slots + 71 * members),
            bytes_accessed=4 * members * (slots + count * members),
            transcendentals=0,
        ),
        name="solve",
    )(live, own, *others, departure, variance, nearest)


def prepare_kernel(blocks, *refs):
    cells, (x_ref, mean_ref) = refs[:blocks], refs[blocks:]
    me = lax.axis_index("mem")
    members = x_ref.shape[3]
    strip = members // blocks
    total = sum(jnp.sum(ref[...], axis=2, keepdims=True) for ref in cells)
    mean = total * (1.0 / members)
    mean_ref[...] = jnp.broadcast_to(mean, mean_ref.shape)
    for shift, ref in enumerate(cells):
        x0, x1 = split2(ref[...] - mean)
        if blocks == 1:
            x_ref[0], x_ref[1] = x0, x1
        else:
            owner = lax.rem(me - shift + blocks, blocks)
            place = pl.ds(pl.multiple_of(owner * strip, strip), strip)
            x_ref[0, :, :, place] = x0
            x_ref[1, :, :, place] = x1


def prepare(cells, part):
    width, height, strip = cells[0].shape
    members = strip * len(cells)
    vmem = pl.BlockSpec(memory_space=pltpu.VMEM)
    return pl.pallas_call(
        functools.partial(prepare_kernel, len(cells)),
        out_shape=[
            jax.ShapeDtypeStruct((2, width, height, members), BF16),
            jax.ShapeDtypeStruct((width, height, part), F32),
        ],
        in_specs=[vmem] * len(cells),
        out_specs=[vmem] * 2,
        compiler_params=pltpu.CompilerParams(
            vmem_limit_bytes=16 * width * height * members + 8 * MIB
        ),
        cost_estimate=pl.CostEstimate(
            flops=8 * width * height * members,
            bytes_accessed=8 * width * height * members,
            transcendentals=0,
        ),
    )(*cells)


def column_intervals(width):
    spacing = width // CGX
    edges = [0] + [spacing * c + spacing // 2 for c in range(CGX)] + [width]
    return list(zip(edges[:-1], edges[1:]))


def window(refs, first):
    return [(ref, first - start) for ref, start in refs if start <= first][-1]


def add_terms(geometry, intervals, x_refs, t_ref, before_refs, out_refs, mine, bands_y=None):
    width, height, bands = geometry
    part = out_refs[0][0].shape[2]
    members = x_refs[0][0].shape[3]
    spacing = width // CGX
    depth = height // bands
    for v in range(bands + 1) if bands_y is None else bands_y:
        j0, j1 = max(depth * v - depth // 2, 0), min(depth * v + depth // 2, height)
        tall = j1 - j0
        j = lax.broadcasted_iota(jnp.int32, (1, tall, 1), 1).astype(F32) + (
            j0 + 0.5 - (v - 0.5) * depth
        )
        upper = j * (1.0 / depth)
        along_y = (1.0 - upper, upper)
        for c in intervals:
            i0, i1 = column_intervals(width)[c]
            wide = i1 - i0
            before, b0 = window(before_refs, i0)
            out, o0 = window(out_refs, i0)
            slots = [(v + a, c + b) for a in (0, 1) for b in (0, 1) if (v + a, c + b) in mine]
            result = before[b0 : b0 + wide, j0:j1, :]
            if slots:
                x, x_first = window(x_refs, i0)
                x0 = x[0, x_first : x_first + wide, j0:j1, :].reshape(wide * tall, members)
                x1 = x[1, x_first : x_first + wide, j0:j1, :].reshape(wide * tall, members)
                left = jnp.concatenate([x0, x0, x1], axis=1)
                i = lax.broadcasted_iota(jnp.int32, (wide, 1, 1), 0).astype(F32) + (
                    i0 + 0.5 - (c - 0.5) * spacing
                )
                right = i * (1.0 / spacing)
                along_x = (1.0 - right, right)
                t0 = jnp.concatenate([t_ref[mine[slot], 0] for slot in slots], axis=0)
                t1 = jnp.concatenate([t_ref[mine[slot], 1] for slot in slots], axis=0)
                product = dot_nt(left, jnp.concatenate([t0, t1, t0], axis=1))
                product = product.reshape(wide, tall, len(slots) * part)
                for n, (row, column) in enumerate(slots):
                    weight = along_x[column - c] * along_y[row - v]
                    result = result + weight * product[:, :, n * part : (n + 1) * part]
            out[o0 : o0 + wide, j0:j1, :] = result


def inner_slots(bands):
    names = [(row, column) for row in range(1, bands + 1) for column in range(1, CGX + 1)]
    return {name: n for n, name in enumerate(names)}


def edge_slots(bands):
    names = [(row, column) for row in (0, bands + 1) for column in (1, CGX)]
    names += [(row, column) for row in range(1, bands + 1) for column in (0, CGX + 1)]
    names += [(row, column) for row in range(1, bands + 1) for column in (CGX - 1, CGX)]
    return {name: n for n, name in enumerate(names)}


def last_slots(bands):
    names = [(row, column) for row in (0, bands + 1) for column in range(2, CGX)]
    return {name: n for n, name in enumerate(names)}


def put(t_ref, slot, value):
    t0, t1 = split2(value)
    t_ref[slot, 0] = t0
    t_ref[slot, 1] = t1


def put_ends(t_ref, south, north, bands, tiles_y, shift, tile_value, end_value):
    me = lax.axis_index("mem")
    tile_y = lax.axis_index("gy")
    band = lax.rem(me - shift + bands, bands)

    @pl.when((tile_y == 0) & (band == 0))
    def _():
        put(t_ref, south, tile_value())

    @pl.when((tile_y == tiles_y - 1) & (band == bands - 1))
    def _():
        put(t_ref, north, tile_value())

    @pl.when((tile_y > 0) & (me == (shift - 1) % bands))
    def _():
        put(t_ref, south, end_value())

    @pl.when((tile_y < tiles_y - 1) & (me == shift))
    def _():
        put(t_ref, north, end_value())


def inner_kernel(geometry, intervals, first, *refs):
    bands = geometry[2]
    x_ref, mean_ref = refs[:2]
    rows = refs[2 : 2 * bands + 1]
    out_ref, t_ref = refs[2 * bands + 1 :]
    me = lax.axis_index("mem")
    for shift in range(bands):
        band = lax.rem(me - shift + bands, bands)
        for n, point in enumerate(POINTS):
            if point + 1 < intervals[0] or point > intervals[-1]:
                continue
            if shift == 0:
                value = rows[0][n]
            elif n < 2:
                value = rows[2 * shift - 1][n]
            else:
                value = rows[2 * shift][n - 2]
            put(t_ref, band * CGX + point, value)
    slots = inner_slots(bands)
    add_terms(
        geometry,
        intervals,
        [(x_ref, first)],
        t_ref,
        [(mean_ref, first)],
        [(out_ref, first)],
        slots,
    )


def edge_kernel(geometry, firsts, tiles_y, *refs):
    refs = list(refs)

    def take(n):
        taken, refs[:n] = refs[:n], []
        return taken

    bands = geometry[2]
    x_refs = list(zip(take(len(firsts)), firsts))
    before_refs = list(zip(take(len(firsts)), firsts))
    rows, ends, mids, sides = take(bands), take(bands), take(bands - 1), take(2)
    out_ref, t_ref = refs
    me = lax.axis_index("mem")
    slots = edge_slots(bands)
    for shift in range(bands):
        band = lax.rem(me - shift + bands, bands)
        for n, point in enumerate(SIDES):
            put_ends(
                t_ref,
                slots[0, point + 1],
                slots[bands + 1, point + 1],
                bands,
                tiles_y,
                shift,
                lambda shift=shift, n=n: rows[shift][n],
                lambda shift=shift, n=n: ends[shift][n],
            )
        for side in (0, 1):
            put(t_ref, slots[1, 0] + 2 * band + side, sides[side][shift])
        for n, point in enumerate(POINTS):
            if (1, point + 1) in slots:
                value = rows[shift][n] if shift == 0 or n < 2 else mids[shift - 1][n - 2]
                put(t_ref, slots[1, CGX - 1] + 2 * band + point + 2 - CGX, value)
    rows_in, columns_in = range(1, bands + 1), range(1, CGX + 1)
    late = {name: n for name, n in slots.items() if not (name[0] in rows_in and name[1] in columns_in)}
    for intervals, mine in ((range(CGX - 1), late), (range(CGX - 1, CGX + 1), slots)):
        add_terms(geometry, intervals, x_refs, t_ref, before_refs, [(out_ref, 0)], mine)


def corner_kernel(bands, tiles_y, spacing, depth, *refs):
    edge_ref = refs[0]
    rows, ends = refs[1 : 1 + bands], refs[1 + bands : 1 + 2 * bands]
    left_ref, right_ref, t_ref = refs[1 + 2 * bands :]
    members = edge_ref.shape[3]
    part = left_ref.shape[2]
    for shift in range(bands):
        for n in (0, 1):
            put_ends(
                t_ref,
                n,
                2 + n,
                bands,
                tiles_y,
                shift,
                lambda shift=shift, n=n: rows[shift][n],
                lambda shift=shift, n=n: ends[shift][n],
            )
    half, tall = spacing // 2, depth // 2
    i = lax.broadcasted_iota(jnp.int32, (half, 1, 1), 0).astype(F32) + 0.5
    j = lax.broadcasted_iota(jnp.int32, (1, tall, 1), 1).astype(F32) + 0.5
    along_x = (i * (1.0 / spacing), 0.5 - i * (1.0 / spacing))
    along_y = (0.5 - j * (1.0 / depth), j * (1.0 / depth))
    for n, out_ref in enumerate((left_ref, right_ref)):
        for end in (0, 1):
            cells = slice(end * tall, (end + 1) * tall)
            first = 0 if n else half
            x0 = edge_ref[0, first : first + half, cells, :].reshape(half * tall, members)
            x1 = edge_ref[1, first : first + half, cells, :].reshape(half * tall, members)
            slot = 2 * end + n
            product = dot_nt(
                jnp.concatenate([x0, x0, x1], axis=1),
                jnp.concatenate([t_ref[slot, 0], t_ref[slot, 1], t_ref[slot, 0]], axis=1),
            )
            out_ref[:, cells, :] = (
                along_x[n] * along_y[end] * product.reshape(half, tall, part)
            )


def corners(bands, tiles_y, spacing, depth, edge, rows, ends):
    part, members = rows[0].shape[1:]
    vmem = pl.BlockSpec(memory_space=pltpu.VMEM)
    shape = jax.ShapeDtypeStruct((spacing // 2, depth, part), F32)
    return pl.pallas_call(
        functools.partial(corner_kernel, bands, tiles_y, spacing, depth),
        out_shape=[shape] * 2,
        in_specs=[vmem] * (1 + 2 * bands),
        out_specs=[vmem] * 2,
        scratch_shapes=[pltpu.VMEM((4, 2, part, members), BF16)],
        compiler_params=pltpu.CompilerParams(vmem_limit_bytes=16 * MIB),
        cost_estimate=pl.CostEstimate(
            flops=12 * spacing * depth * part * members,
            bytes_accessed=16 * part * members,
            transcendentals=0,
        ),
        name="corners",
    )(edge, *rows, *ends)


def last_kernel(geometry, firsts, tiles_y, *refs):
    refs = list(refs)

    def take(n):
        taken, refs[:n] = refs[:n], []
        return taken

    width, height, bands = geometry
    x_refs = list(zip(take(len(firsts)), firsts))
    (before_ref,) = take(1)
    rows, ends, given = take(bands), take(bands), take(2)
    out_ref, t_ref, result_ref, sems = refs
    slots = last_slots(bands)
    half, depth, _ = given[0].shape
    tall = depth // 2

    def leave(from_ref, start, stop, sem):
        place = slice(start, stop)
        return pltpu.make_async_copy(
            from_ref.at[:, place, :], out_ref.at[:, place, :], sems.at[sem]
        )

    middle = leave(before_ref, tall, height - tall, 0)
    middle.start()
    for shift in range(bands):
        for n in range(CGX - 2):
            k = 2 + n if shift == 0 else n
            put_ends(
                t_ref,
                slots[0, 2 + n],
                slots[bands + 1, 2 + n],
                bands,
                tiles_y,
                shift,
                lambda shift=shift, k=k: rows[shift][k],
                lambda shift=shift, k=k: ends[shift][k],
            )
    copies = [middle]
    for end, (v, j) in enumerate(((0, 0), (bands, height - tall))):
        add_terms(
            geometry,
            range(CGX + 1),
            x_refs,
            t_ref,
            [(before_ref, 0)],
            [(result_ref, 0)],
            slots,
            (v,),
        )
        for ref, first in zip(given, (0, width - half)):
            result_ref[first : first + half, j : j + tall, :] = (
                before_ref[first : first + half, j : j + tall, :]
                + ref[:, end * tall : (end + 1) * tall, :]
            )
        copies.append(leave(result_ref, j, j + tall, end + 1))
        copies[-1].start()
    for copy in copies:
        copy.wait()


def apply_terms(kernel, width, xs, befores, operands, slots, flops, copies=False):
    _, _, height, members = xs[0].shape
    part = befores[0].shape[2]
    vmem = pl.BlockSpec(memory_space=pltpu.VMEM)
    operands = list(xs) + list(befores) + list(operands)
    size = sum(array.size * array.dtype.itemsize for array in operands)
    return pl.pallas_call(
        kernel,
        out_shape=jax.ShapeDtypeStruct((width, height, part), F32),
        in_specs=[vmem] * len(operands),
        out_specs=pl.BlockSpec(memory_space=pl.ANY) if copies else vmem,
        scratch_shapes=[pltpu.VMEM((len(slots), 2, part, members), BF16)]
        + [pltpu.VMEM((width, height, part), F32), pltpu.SemaphoreType.DMA((3,))] * copies,
        compiler_params=pltpu.CompilerParams(
            vmem_limit_bytes=min(size + 8 * width * height * part + 16 * MIB, 60 * MIB)
        ),
        cost_estimate=pl.CostEstimate(
            flops=flops, bytes_accessed=size, transcendentals=0
        ),
    )(*operands)


def shifted(array, axis, by):
    size = lax.axis_size(axis)
    return lax.ppermute(array, axis, [(i, (i + by) % size) for i in range(size)])


def to_next_tile(array, shift):
    bands = lax.axis_size("mem")
    tiles = lax.axis_size("gy")
    last, first = (shift - 1) % bands, shift
    pairs = [(last * tiles + y, last * tiles + y + 1) for y in range(tiles - 1)]
    pairs += [(first * tiles + y, first * tiles + y - 1) for y in range(1, tiles)]
    return lax.ppermute(array, ("mem", "gy"), pairs)


def analysis(background, anomalies, departure, variance, nearest, tally):
    bands = lax.axis_size("mem")
    tiles_y = lax.axis_size("gy")
    me = lax.axis_index("mem")
    part = background.shape[0]
    members = part * bands
    slots = departure.shape[3]

    def of_band(band):
        return lax.dynamic_slice_in_dim(anomalies, band * slots, slots, axis=3)

    others = [of_band(lax.rem(me + shift, bands)) for shift in range(1, bands)]
    anomalies, others = lax.optimization_barrier((anomalies, others))
    others = [shifted(piece.reshape(part, slots), "mem", s) for s, piece in enumerate(others, 1)]
    own = of_band(me).reshape(part, slots)
    tile = background.transpose(1, 2, 0)
    width, height = tile.shape[:2]
    spacing, depth = width // CGX, height // bands
    ends_y = jnp.concatenate([tile[:, : depth // 2], tile[:, height - depth // 2 :]], axis=1)
    edge = jnp.concatenate(
        [
            shifted(ends_y[: spacing // 2], "gx", -1),
            shifted(ends_y[width - spacing // 2 :], "gx", 1),
        ],
        axis=0,
    )

    def gathered(array):
        blocks = [array]
        for shift in range(1, bands):
            blocks.append(shifted(array, "mem", shift))
        if part % 128:
            order = lax.rem(me - jnp.arange(bands) + bands, bands)
            blocks = jnp.take(jnp.stack(blocks, axis=2), order, axis=2)
            blocks = [blocks.reshape(blocks.shape[:2] + (members,))]
        return blocks

    firsts = (0, column_intervals(width)[CGX - 1][0])
    second = tile[firsts[1] :]
    cells = [gathered(tile[: firsts[1]]), gathered(second)]
    edges = gathered(edge)
    solved = solve(
        POINTS,
        tally.reshape(1),
        own,
        others,
        departure.reshape(1, slots),
        variance.reshape(1, slots),
        nearest.reshape(1, slots),
    )
    row = solved[0]
    other_side = [shifted(solved[2 * s - 1], "mem", s) for s in range(1, bands)]
    other_mid = [shifted(solved[2 * s], "mem", s) for s in range(1, bands)]
    own_end = to_next_tile(row, 0)
    ends_side = [to_next_tile(other_side[s - 1], s) for s in range(1, bands)]
    row_sides = [
        shifted(jnp.stack([row[n]] + [array[n] for array in other_side]), "gx", by)
        for n, by in ((1, 1), (0, -1))
    ]
    ends_mid = [to_next_tile(other_mid[s - 1], s) for s in range(1, bands)]
    geometry = (width, height, bands)
    edge, _ = prepare(edges, part)
    x_first, mean_first = prepare(cells[0], part)
    left, right = corners(
        bands, tiles_y, spacing, depth, edge, [row] + other_side, [own_end] + ends_side
    )
    given = [shifted(right, "gx", 1), shifted(left, "gx", -1)]
    operands = [row]
    for side, mid in zip(other_side, other_mid):
        operands += [side, mid]
    work = 6 * width * height * part * members

    def inner(x, mean, intervals, first):
        return apply_terms(
            functools.partial(inner_kernel, geometry, intervals, first),
            x.shape[1],
            [x],
            [mean],
            operands,
            inner_slots(bands),
            3 * work * x.shape[1] // width,
        )

    inner_first = inner(x_first, mean_first, range(CGX - 1), 0)
    x_second, mean_second = prepare(cells[1], part)
    xs = [x_first, x_second]
    result = apply_terms(
        functools.partial(edge_kernel, geometry, firsts, tiles_y),
        width,
        xs,
        [inner_first, mean_second],
        [row] + other_side + [own_end] + ends_side + other_mid + row_sides,
        edge_slots(bands),
        work,
    )
    result = apply_terms(
        functools.partial(last_kernel, geometry, firsts, tiles_y),
        width,
        xs,
        [result],
        [row] + other_mid + [own_end] + ends_mid + given,
        last_slots(bands),
        work // 2,
        copies=True,
    )
    return result.transpose(2, 0, 1)


def solution(mesh):
    in_specs = (
        P("mem", "gx", "gy"),
        P("mem", "gx", "gy", None),
        P("gx", "gy", "mem", None),
        P("gx", "gy", "mem", None),
        P("gx", "gy", "mem", None),
        P("gx", "gy", "mem"),
    )
    out_specs = P("mem", "gx", "gy")
    return jax.shard_map(
        analysis, mesh=mesh, in_specs=in_specs, out_specs=out_specs, check_vma=False
    )
```

```python
import functools

import jax
import jax.numpy as jnp
from jax import lax
from jax.experimental import pallas as pl
from jax.experimental.pallas import tpu as pltpu
from jax.sharding import PartitionSpec as P


CGX = 4
NS_STEPS = 12
SIDES = (0, CGX - 1)
POINTS = SIDES + tuple(range(1, CGX - 1))

F32 = jnp.float32
BF16 = jnp.bfloat16
MIB = 1024 * 1024
NT = (((1,), (1,)), ((), ()))


def dot(a, b):
    return jnp.dot(a, b, preferred_element_type=F32)


def dot_nt(a, b):
    return lax.dot_general(a, b, NT, preferred_element_type=F32)


def split2(x):
    high = x.astype(BF16)
    return high, (x - high.astype(F32)).astype(BF16)


def split3(x):
    high = x.astype(BF16)
    rest = x - high.astype(F32)
    mid = rest.astype(BF16)
    return high, mid, (rest - mid.astype(F32)).astype(BF16)


def mm3(a, b):
    n = a[0].shape[0]
    both = dot(jnp.concatenate([a[0], a[1]], axis=0), b[0])
    return both[:n] + (both[n:] + dot(a[0], b[1]))


def mm5(a, b):
    n = a[0].shape[0]
    three = dot(jnp.concatenate([a[0], a[1], a[2]], axis=0), b[0])
    two = dot(jnp.concatenate([a[0], a[1]], axis=0), b[1])
    return three[:n] + ((three[n : 2 * n] + two[:n]) + (three[2 * n :] + two[n:]))


def mm1(a, b):
    return dot(a[0], b[0])


def quartics(ps, identity, square_mm, inner_mm):
    squares = [square_mm(piece, piece) for piece in [split2(p) for p in ps]]
    inner = [
        inner_mm(split2(square), split2(0.0625 * square - 0.5625 * p))
        for p, square in zip(ps, squares)
    ]
    return [
        split2(product + (1.6875 * square + (2.25 * identity - 2.4375 * p)))
        for p, square, product in zip(ps, squares, inner)
    ]


def solve_kernel(points, bands, live_ref, own_ref, *refs):
    others = refs[: bands - 1]
    departure_ref, variance_ref, nearest_ref = refs[bands - 1 : bands + 2]
    outs = refs[bands + 2 : 3 * bands + 1]
    y_ref, z_ref, cov_ref, right_ref, root_ref, inv_ref = refs[3 * bands + 1 :]
    me = lax.axis_index("mem")
    part, slots = own_ref.shape
    members = y_ref.shape[0]
    for shift, ref in enumerate((own_ref,) + tuple(others)):
        owner = lax.rem(me - shift + bands, bands)
        y_ref[pl.ds(pl.multiple_of(owner * part, part), part), :] = ref[...]
    rows = lax.broadcasted_iota(jnp.int32, (members, members), 0)
    columns = lax.broadcasted_iota(jnp.int32, (members, members), 1)
    identity = (rows == columns).astype(F32)
    live = (lax.broadcasted_iota(jnp.int32, (1, slots), 1) < live_ref[0]).astype(F32)
    base = live * lax.rsqrt(variance_ref[...])
    scales, roots, sums = [], [], []
    count = len(points)

    def split(g):
        distance = (nearest_ref[...] - points[g]).astype(F32)
        weight = jnp.exp(-0.25 * distance * distance) * base
        y0, y1 = split2(y_ref[...] * weight)
        d0, d1 = split2(weight * departure_ref[...])
        z_ref[g, :members], z_ref[g, members : 2 * members] = y0, y1
        z_ref[g, 2 * members :] = jnp.concatenate(
            [jnp.broadcast_to(d0, (16, slots)), jnp.broadcast_to(d1, (16, slots))], axis=0
        )

    split(0)
    for g in range(count):
        first = dot_nt(z_ref[g], z_ref[g, :members])
        if g + 1 < count:
            split(g + 1)
        second = dot_nt(z_ref[g, members : 2 * members + 16], z_ref[g, members : 2 * members])
        sums.append((first, second))
    for first, second in sums:
        cross = first[members : 2 * members]
        cov = first[:members] + second[:members] + (cross + cross.T)
        cov = cov + (members - 1.0) * identity
        right = first[2 * members :]
        right_ref[len(roots)] = right[:8] + right[16:24] + second[members : members + 8]
        square_sum = jnp.sum(jnp.sum(cov * cov, axis=1, keepdims=True), axis=0, keepdims=True)
        scale = lax.rsqrt(square_sum)
        scales.append(scale)
        roots.append(cov * scale)
    us = quartics(roots, identity, mm1, mm1)
    for g in range(count):
        for i, piece in enumerate(split3(mm5(split3(roots[g]), us[g]))):
            root_ref[g, i] = piece
        inv_ref[g, 0], inv_ref[g, 1] = us[g]

    def products():
        return [
            mm3((inv_ref[g, 0], inv_ref[g, 1]), (root_ref[g, 0], root_ref[g, 1]))
            for g in range(count)
        ]

    def inverses(us):
        return [mm3(us[g], (inv_ref[g, 0], inv_ref[g, 1])) for g in range(count)]

    def step(square_mm, full):
        us = quartics(products(), identity, square_mm, mm1)
        if full:
            new = [
                mm5((root_ref[g, 0], root_ref[g, 1], root_ref[g, 2]), us[g])
                for g in range(count)
            ]
        else:
            new = [mm3((root_ref[g, 0], root_ref[g, 1]), us[g]) for g in range(count)]
        for g in range(count):
            pieces = split3(new[g]) if full else split2(new[g])
            for i, piece in enumerate(pieces):
                root_ref[g, i] = piece
        new = inverses(us)
        for g in range(count):
            inv_ref[g, 0], inv_ref[g, 1] = split2(new[g])

    def early(_, carry):
        step(mm1, True)
        return carry

    lax.fori_loop(0, NS_STEPS // 2 - 3, early, 0)
    step(mm3, False)
    lasts = inverses(quartics(products(), identity, mm3, mm3))
    for g in range(count):
        last = lasts[g]
        right = right_ref[g, 0:1, :]
        half = jnp.sum(last * right, axis=1, keepdims=True)
        mean_weights = jnp.sum(last * half, axis=0, keepdims=True) * scales[g]
        cov_ref[...] = last * jnp.sqrt((members - 1.0) * scales[g]) + mean_weights
        for shift in range(bands):
            target = lax.rem(me + shift, bands)
            rows = cov_ref[pl.ds(pl.multiple_of(target * part, part), part), :]
            if shift == 0:
                outs[0][g] = rows
            elif g < 2:
                outs[2 * shift - 1][g] = rows
            else:
                outs[2 * shift][g - 2] = rows


def solve(points, live, own, others, departure, variance, nearest):
    bands = 1 + len(others)
    part, slots = own.shape
    members = part * bands
    count = len(points)
    vmem = pl.BlockSpec(memory_space=pltpu.VMEM)
    return pl.pallas_call(
        functools.partial(solve_kernel, points, bands),
        out_shape=[jax.ShapeDtypeStruct((count, part, members), F32)]
        + [
            jax.ShapeDtypeStruct((n, part, members), F32)
            for _ in others
            for n in (2, count - 2)
        ],
        in_specs=[pl.BlockSpec(memory_space=pltpu.SMEM)] + [vmem] * (bands + 3),
        out_specs=[vmem] * (2 * bands - 1),
        scratch_shapes=[
            pltpu.VMEM((members, slots), F32),
            pltpu.VMEM((count, 2 * members + 32, slots), BF16),
            pltpu.VMEM((members, members), F32),
            pltpu.VMEM((count, 8, members), F32),
            pltpu.VMEM((count, 3, members, members), BF16),
            pltpu.VMEM((count, 2, members, members), BF16),
        ],
        compiler_params=pltpu.CompilerParams(vmem_limit_bytes=32 * MIB),
        cost_estimate=pl.CostEstimate(
            flops=2 * count * members * members * (3 * slots + 71 * members),
            bytes_accessed=4 * members * (slots + count * members),
            transcendentals=0,
        ),
        name="solve",
    )(live, own, *others, departure, variance, nearest)


def prepare_kernel(blocks, *refs):
    cells, (x_ref, mean_ref) = refs[:blocks], refs[blocks:]
    me = lax.axis_index("mem")
    members = x_ref.shape[3]
    strip = members // blocks
    total = sum(jnp.sum(ref[...], axis=2, keepdims=True) for ref in cells)
    mean = total * (1.0 / members)
    mean_ref[...] = jnp.broadcast_to(mean, mean_ref.shape)
    for shift, ref in enumerate(cells):
        x0, x1 = split2(ref[...] - mean)
        if blocks == 1:
            x_ref[0], x_ref[1] = x0, x1
        else:
            owner = lax.rem(me - shift + blocks, blocks)
            place = pl.ds(pl.multiple_of(owner * strip, strip), strip)
            x_ref[0, :, :, place] = x0
            x_ref[1, :, :, place] = x1


def prepare(cells, part):
    width, height, strip = cells[0].shape
    members = strip * len(cells)
    vmem = pl.BlockSpec(memory_space=pltpu.VMEM)
    return pl.pallas_call(
        functools.partial(prepare_kernel, len(cells)),
        out_shape=[
            jax.ShapeDtypeStruct((2, width, height, members), BF16),
            jax.ShapeDtypeStruct((width, height, part), F32),
        ],
        in_specs=[vmem] * len(cells),
        out_specs=[vmem] * 2,
        compiler_params=pltpu.CompilerParams(
            vmem_limit_bytes=16 * width * height * members + 8 * MIB
        ),
        cost_estimate=pl.CostEstimate(
            flops=8 * width * height * members,
            bytes_accessed=8 * width * height * members,
            transcendentals=0,
        ),
    )(*cells)


def column_intervals(width):
    spacing = width // CGX
    edges = [0] + [spacing * c + spacing // 2 for c in range(CGX)] + [width]
    return list(zip(edges[:-1], edges[1:]))


def window(refs, first):
    return [(ref, first - start) for ref, start in refs if start <= first][-1]


def add_terms(geometry, intervals, x_refs, t_ref, before_refs, out_refs, mine, bands_y=None):
    width, height, bands = geometry
    part = out_refs[0][0].shape[2]
    members = x_refs[0][0].shape[3]
    spacing = width // CGX
    depth = height // bands
    for v in range(bands + 1) if bands_y is None else bands_y:
        j0, j1 = max(depth * v - depth // 2, 0), min(depth * v + depth // 2, height)
        tall = j1 - j0
        j = lax.broadcasted_iota(jnp.int32, (1, tall, 1), 1).astype(F32) + (
            j0 + 0.5 - (v - 0.5) * depth
        )
        upper = j * (1.0 / depth)
        along_y = (1.0 - upper, upper)
        for c in intervals:
            i0, i1 = column_intervals(width)[c]
            wide = i1 - i0
            before, b0 = window(before_refs, i0)
            out, o0 = window(out_refs, i0)
            slots = [(v + a, c + b) for a in (0, 1) for b in (0, 1) if (v + a, c + b) in mine]
            result = before[b0 : b0 + wide, j0:j1, :]
            if slots:
                x, x_first = window(x_refs, i0)
                x0 = x[0, x_first : x_first + wide, j0:j1, :].reshape(wide * tall, members)
                x1 = x[1, x_first : x_first + wide, j0:j1, :].reshape(wide * tall, members)
                left = jnp.concatenate([x0, x0, x1], axis=1)
                i = lax.broadcasted_iota(jnp.int32, (wide, 1, 1), 0).astype(F32) + (
                    i0 + 0.5 - (c - 0.5) * spacing
                )
                right = i * (1.0 / spacing)
                along_x = (1.0 - right, right)
                t0 = jnp.concatenate([t_ref[mine[slot], 0] for slot in slots], axis=0)
                t1 = jnp.concatenate([t_ref[mine[slot], 1] for slot in slots], axis=0)
                product = dot_nt(left, jnp.concatenate([t0, t1, t0], axis=1))
                product = product.reshape(wide, tall, len(slots) * part)
                for n, (row, column) in enumerate(slots):
                    weight = along_x[column - c] * along_y[row - v]
                    result = result + weight * product[:, :, n * part : (n + 1) * part]
            out[o0 : o0 + wide, j0:j1, :] = result


def inner_slots(bands):
    names = [(row, column) for row in range(1, bands + 1) for column in range(1, CGX + 1)]
    return {name: n for n, name in enumerate(names)}


def edge_slots(bands):
    names = [(row, column) for row in (0, bands + 1) for column in (1, CGX)]
    names += [(row, column) for row in range(1, bands + 1) for column in (0, CGX + 1)]
    names += [(row, column) for row in range(1, bands + 1) for column in (CGX - 1, CGX)]
    return {name: n for n, name in enumerate(names)}


def last_slots(bands):
    names = [(row, column) for row in (0, bands + 1) for column in range(2, CGX)]
    return {name: n for n, name in enumerate(names)}


def put(t_ref, slot, value):
    t0, t1 = split2(value)
    t_ref[slot, 0] = t0
    t_ref[slot, 1] = t1


def put_ends(t_ref, south, north, bands, tiles_y, shift, tile_value, end_value):
    me = lax.axis_index("mem")
    tile_y = lax.axis_index("gy")
    band = lax.rem(me - shift + bands, bands)

    @pl.when((tile_y == 0) & (band == 0))
    def _():
        put(t_ref, south, tile_value())

    @pl.when((tile_y == tiles_y - 1) & (band == bands - 1))
    def _():
        put(t_ref, north, tile_value())

    @pl.when((tile_y > 0) & (me == (shift - 1) % bands))
    def _():
        put(t_ref, south, end_value())

    @pl.when((tile_y < tiles_y - 1) & (me == shift))
    def _():
        put(t_ref, north, end_value())


def inner_kernel(geometry, intervals, first, *refs):
    bands = geometry[2]
    x_ref, mean_ref = refs[:2]
    rows = refs[2 : 2 * bands + 1]
    out_ref, t_ref = refs[2 * bands + 1 :]
    me = lax.axis_index("mem")
    for shift in range(bands):
        band = lax.rem(me - shift + bands, bands)
        for n, point in enumerate(POINTS):
            if point + 1 < intervals[0] or point > intervals[-1]:
                continue
            if shift == 0:
                value = rows[0][n]
            elif n < 2:
                value = rows[2 * shift - 1][n]
            else:
                value = rows[2 * shift][n - 2]
            put(t_ref, band * CGX + point, value)
    slots = inner_slots(bands)
    add_terms(
        geometry,
        intervals,
        [(x_ref, first)],
        t_ref,
        [(mean_ref, first)],
        [(out_ref, first)],
        slots,
    )


def edge_kernel(geometry, firsts, tiles_y, *refs):
    refs = list(refs)

    def take(n):
        taken, refs[:n] = refs[:n], []
        return taken

    bands = geometry[2]
    x_refs = list(zip(take(len(firsts)), firsts))
    before_refs = list(zip(take(len(firsts)), firsts))
    rows, ends, mids, sides = take(bands), take(bands), take(bands - 1), take(2)
    out_ref, t_ref = refs
    me = lax.axis_index("mem")
    slots = edge_slots(bands)
    for shift in range(bands):
        band = lax.rem(me - shift + bands, bands)
        for n, point in enumerate(SIDES):
            put_ends(
                t_ref,
                slots[0, point + 1],
                slots[bands + 1, point + 1],
                bands,
                tiles_y,
                shift,
                lambda shift=shift, n=n: rows[shift][n],
                lambda shift=shift, n=n: ends[shift][n],
            )
        for side in (0, 1):
            put(t_ref, slots[1, 0] + 2 * band + side, sides[side][shift])
        for n, point in enumerate(POINTS):
            if (1, point + 1) in slots:
                value = rows[shift][n] if shift == 0 or n < 2 else mids[shift - 1][n - 2]
                put(t_ref, slots[1, CGX - 1] + 2 * band + point + 2 - CGX, value)
    rows_in, columns_in = range(1, bands + 1), range(1, CGX + 1)
    late = {name: n for name, n in slots.items() if not (name[0] in rows_in and name[1] in columns_in)}
    for intervals, mine in ((range(CGX - 1), late), (range(CGX - 1, CGX + 1), slots)):
        add_terms(geometry, intervals, x_refs, t_ref, before_refs, [(out_ref, 0)], mine)


def corner_kernel(bands, tiles_y, spacing, depth, *refs):
    edge_ref = refs[0]
    rows, ends = refs[1 : 1 + bands], refs[1 + bands : 1 + 2 * bands]
    left_ref, right_ref, t_ref = refs[1 + 2 * bands :]
    members = edge_ref.shape[3]
    part = left_ref.shape[2]
    for shift in range(bands):
        for n in (0, 1):
            put_ends(
                t_ref,
                n,
                2 + n,
                bands,
                tiles_y,
                shift,
                lambda shift=shift, n=n: rows[shift][n],
                lambda shift=shift, n=n: ends[shift][n],
            )
    half, tall = spacing // 2, depth // 2
    i = lax.broadcasted_iota(jnp.int32, (half, 1, 1), 0).astype(F32) + 0.5
    j = lax.broadcasted_iota(jnp.int32, (1, tall, 1), 1).astype(F32) + 0.5
    along_x = (i * (1.0 / spacing), 0.5 - i * (1.0 / spacing))
    along_y = (0.5 - j * (1.0 / depth), j * (1.0 / depth))
    for n, out_ref in enumerate((left_ref, right_ref)):
        for end in (0, 1):
            cells = slice(end * tall, (end + 1) * tall)
            first = 0 if n else half
            x0 = edge_ref[0, first : first + half, cells, :].reshape(half * tall, members)
            x1 = edge_ref[1, first : first + half, cells, :].reshape(half * tall, members)
            slot = 2 * end + n
            product = dot_nt(
                jnp.concatenate([x0, x0, x1], axis=1),
                jnp.concatenate([t_ref[slot, 0], t_ref[slot, 1], t_ref[slot, 0]], axis=1),
            )
            out_ref[:, cells, :] = (
                along_x[n] * along_y[end] * product.reshape(half, tall, part)
            )


def corners(bands, tiles_y, spacing, depth, edge, rows, ends):
    part, members = rows[0].shape[1:]
    vmem = pl.BlockSpec(memory_space=pltpu.VMEM)
    shape = jax.ShapeDtypeStruct((spacing // 2, depth, part), F32)
    return pl.pallas_call(
        functools.partial(corner_kernel, bands, tiles_y, spacing, depth),
        out_shape=[shape] * 2,
        in_specs=[vmem] * (1 + 2 * bands),
        out_specs=[vmem] * 2,
        scratch_shapes=[pltpu.VMEM((4, 2, part, members), BF16)],
        compiler_params=pltpu.CompilerParams(vmem_limit_bytes=16 * MIB),
        cost_estimate=pl.CostEstimate(
            flops=12 * spacing * depth * part * members,
            bytes_accessed=16 * part * members,
            transcendentals=0,
        ),
        name="corners",
    )(edge, *rows, *ends)


def last_kernel(geometry, firsts, tiles_y, *refs):
    refs = list(refs)

    def take(n):
        taken, refs[:n] = refs[:n], []
        return taken

    width, height, bands = geometry
    x_refs = list(zip(take(len(firsts)), firsts))
    (before_ref,) = take(1)
    rows, ends, given = take(bands), take(bands), take(2)
    out_ref, t_ref, result_ref, sems = refs
    slots = last_slots(bands)
    half, depth, _ = given[0].shape
    tall = depth // 2

    def leave(from_ref, start, stop, sem):
        place = slice(start, stop)
        return pltpu.make_async_copy(
            from_ref.at[:, place, :], out_ref.at[:, place, :], sems.at[sem]
        )

    middle = leave(before_ref, tall, height - tall, 0)
    middle.start()
    for shift in range(bands):
        for n in range(CGX - 2):
            k = 2 + n if shift == 0 else n
            put_ends(
                t_ref,
                slots[0, 2 + n],
                slots[bands + 1, 2 + n],
                bands,
                tiles_y,
                shift,
                lambda shift=shift, k=k: rows[shift][k],
                lambda shift=shift, k=k: ends[shift][k],
            )
    copies = [middle]
    for end, (v, j) in enumerate(((0, 0), (bands, height - tall))):
        add_terms(
            geometry,
            range(CGX + 1),
            x_refs,
            t_ref,
            [(before_ref, 0)],
            [(result_ref, 0)],
            slots,
            (v,),
        )
        for ref, first in zip(given, (0, width - half)):
            result_ref[first : first + half, j : j + tall, :] = (
                before_ref[first : first + half, j : j + tall, :]
                + ref[:, end * tall : (end + 1) * tall, :]
            )
        copies.append(leave(result_ref, j, j + tall, end + 1))
        copies[-1].start()
    for copy in copies:
        copy.wait()


def apply_terms(kernel, width, xs, befores, operands, slots, flops, copies=False):
    _, _, height, members = xs[0].shape
    part = befores[0].shape[2]
    vmem = pl.BlockSpec(memory_space=pltpu.VMEM)
    operands = list(xs) + list(befores) + list(operands)
    size = sum(array.size * array.dtype.itemsize for array in operands)
    return pl.pallas_call(
        kernel,
        out_shape=jax.ShapeDtypeStruct((width, height, part), F32),
        in_specs=[vmem] * len(operands),
        out_specs=pl.BlockSpec(memory_space=pl.ANY) if copies else vmem,
        scratch_shapes=[pltpu.VMEM((len(slots), 2, part, members), BF16)]
        + [pltpu.VMEM((width, height, part), F32), pltpu.SemaphoreType.DMA((3,))] * copies,
        compiler_params=pltpu.CompilerParams(
            vmem_limit_bytes=min(size + 8 * width * height * part + 16 * MIB, 60 * MIB)
        ),
        cost_estimate=pl.CostEstimate(
            flops=flops, bytes_accessed=size, transcendentals=0
        ),
    )(*operands)


def shifted(array, axis, by):
    size = lax.axis_size(axis)
    return lax.ppermute(array, axis, [(i, (i + by) % size) for i in range(size)])


def to_next_tile(array, shift):
    bands = lax.axis_size("mem")
    tiles = lax.axis_size("gy")
    last, first = (shift - 1) % bands, shift
    pairs = [(last * tiles + y, last * tiles + y + 1) for y in range(tiles - 1)]
    pairs += [(first * tiles + y, first * tiles + y - 1) for y in range(1, tiles)]
    return lax.ppermute(array, ("mem", "gy"), pairs)


def analysis(background, anomalies, departure, variance, nearest, tally):
    bands = lax.axis_size("mem")
    tiles_y = lax.axis_size("gy")
    me = lax.axis_index("mem")
    part = background.shape[0]
    members = part * bands
    slots = departure.shape[3]

    def of_band(band):
        return lax.dynamic_slice_in_dim(anomalies, band * slots, slots, axis=3)

    others = [of_band(lax.rem(me + shift, bands)) for shift in range(1, bands)]
    anomalies, others = lax.optimization_barrier((anomalies, others))
    others = [shifted(piece.reshape(part, slots), "mem", s) for s, piece in enumerate(others, 1)]
    own = of_band(me).reshape(part, slots)
    tile = background.transpose(1, 2, 0)
    width, height = tile.shape[:2]
    spacing, depth = width // CGX, height // bands
    ends_y = jnp.concatenate([tile[:, : depth // 2], tile[:, height - depth // 2 :]], axis=1)
    edge = jnp.concatenate(
        [
            shifted(ends_y[: spacing // 2], "gx", -1),
            shifted(ends_y[width - spacing // 2 :], "gx", 1),
        ],
        axis=0,
    )

    def gathered(array):
        blocks = [array]
        for shift in range(1, bands):
            blocks.append(shifted(array, "mem", shift))
        if part % 128:
            order = lax.rem(me - jnp.arange(bands) + bands, bands)
            blocks = jnp.take(jnp.stack(blocks, axis=2), order, axis=2)
            blocks = [blocks.reshape(blocks.shape[:2] + (members,))]
        return blocks

    firsts = (0, column_intervals(width)[CGX - 1][0])
    second = tile[firsts[1] :]
    cells = [gathered(tile[: firsts[1]]), gathered(second)]
    edges = gathered(edge)
    solved = solve(
        POINTS,
        tally.reshape(1),
        own,
        others,
        departure.reshape(1, slots),
        variance.reshape(1, slots),
        nearest.reshape(1, slots),
    )
    row = solved[0]
    other_side = [shifted(solved[2 * s - 1], "mem", s) for s in range(1, bands)]
    other_mid = [shifted(solved[2 * s], "mem", s) for s in range(1, bands)]
    own_end = to_next_tile(row, 0)
    ends_side = [to_next_tile(other_side[s - 1], s) for s in range(1, bands)]
    row_sides = [
        shifted(jnp.stack([row[n]] + [array[n] for array in other_side]), "gx", by)
        for n, by in ((1, 1), (0, -1))
    ]
    ends_mid = [to_next_tile(other_mid[s - 1], s) for s in range(1, bands)]
    geometry = (width, height, bands)
    edge, _ = prepare(edges, part)
    x_first, mean_first = prepare(cells[0], part)
    left, right = corners(
        bands, tiles_y, spacing, depth, edge, [row] + other_side, [own_end] + ends_side
    )
    given = [shifted(right, "gx", 1), shifted(left, "gx", -1)]
    operands = [row]
    for side, mid in zip(other_side, other_mid):
        operands += [side, mid]
    work = 6 * width * height * part * members

    def inner(x, mean, intervals, first):
        return apply_terms(
            functools.partial(inner_kernel, geometry, intervals, first),
            x.shape[1],
            [x],
            [mean],
            operands,
            inner_slots(bands),
            3 * work * x.shape[1] // width,
        )

    inner_first = inner(x_first, mean_first, range(CGX - 1), 0)
    x_second, mean_second = prepare(cells[1], part)
    xs = [x_first, x_second]
    result = apply_terms(
        functools.partial(edge_kernel, geometry, firsts, tiles_y),
        width,
        xs,
        [inner_first, mean_second],
        [row] + other_side + [own_end] + ends_side + other_mid + row_sides,
        edge_slots(bands),
        work,
    )
    result = apply_terms(
        functools.partial(last_kernel, geometry, firsts, tiles_y),
        width,
        xs,
        [result],
        [row] + other_mid + [own_end] + ends_mid + given,
        last_slots(bands),
        work // 2,
        copies=True,
    )
    return result.transpose(2, 0, 1)


def solution(mesh):
    in_specs = (
        P("mem", "gx", "gy"),
        P("mem", "gx", "gy", None),
        P("gx", "gy", "mem", None),
        P("gx", "gy", "mem", None),
        P("gx", "gy", "mem", None),
        P("gx", "gy", "mem"),
    )
    out_specs = P("mem", "gx", "gy")
    return jax.shard_map(
        analysis, mesh=mesh, in_specs=in_specs, out_specs=out_specs, check_vma=False
    )
```
